32 devices in a mesh: tm: 4 (over z), space: 8 (over y, x, core).
Axes of the slice: x: 2, y: 2, z: 4, core: 2. Of those that a mesh axis runs over, the one named last changes fastest.
Arguments:
- c_state: float32 [4, 2, 64, 2048], P('tm', None, 'space'), may hold values from -4 to 4
Outputs:
- next_state: float32 [4, 2, 64, 2048], P('tm', None, 'space')
The draws below stay inside these ranges and needn't reach their ends.
All inputs are finite; a program needn't handle non-finite values.
Results may differ from the reference program's by a relative error of at most 0.00002.
Values sent between devices are 32-bit elements; how exact they have to be, the bound alone decides.
No kernel may reach another device: no remote copies, remote signals or barrier semaphores. Data moves between devices by JAX's collectives and lax.ppermute only.
A program may use at most 64 MiB of HBM per device.

```python
import jax
import jax.numpy as jnp
from jax import lax

NY = 2048
FSTEPS = 4
CF = 4
GROUPS = 4
NX = 64


def block_scale(rng, extent, pieces, least, high):
    level, own = 1.0, jax.random.fold_in(rng, 6)
    for position, blocks in pieces:
        draws = jnp.exp(jax.random.uniform(jax.random.fold_in(own, position), (blocks,), jnp.float32, least / len(pieces), high / len(pieces)))
        level = level * jnp.repeat(draws, extent[position] // blocks).reshape([-1 if axis == position else 1 for axis in range(len(extent))])
    return level


def centred(rng, extent, scale, reach, cuts=(), dtype=jnp.bfloat16):
    level = block_scale(rng, extent, cuts, -0.22, 0.18) if cuts else 1.0
    array = jax.random.normal(rng, extent, jnp.float32) * scale * level
    return jnp.minimum(jnp.maximum(array, -reach), reach).astype(dtype)


def setup_inputs(seed: int = 0) -> dict:
    key_of = jax.random.split(jax.random.key(seed), 2)
    c_state = centred(key_of[0], (GROUPS, 2, NX, NY), 1.0, 4.0, ((0, 4), (2, 8)), jnp.float32)
    return dict(c_state=c_state)


COURANT = 0.06
DIFFUSION = 0.04


def advance(padded, courant, diffusion):
    center = padded[:, 1:-1]
    row_above = padded[:, :-2]
    row_below = padded[:, 2:]
    col_left = jnp.roll(center, 1, axis=2)
    col_right = jnp.roll(center, -1, axis=2)
    along_u = center[0:1]
    along_v = center[1:2]
    transport = jnp.maximum(along_u, 0.0) * (center - row_above) + jnp.minimum(along_u, 0.0) * (row_below - center)
    transport = transport + jnp.maximum(along_v, 0.0) * (center - col_left) + jnp.minimum(along_v, 0.0) * (col_right - center)
    spread = row_above + row_below + col_left + col_right - 4.0 * center
    return center - courant * transport + diffusion * spread


def wrap_rows(field):
    return jnp.concatenate([field[:, -1:], field, field[:, :1]], axis=1)


def restrict(field):
    blocks = field.reshape(field.shape[0], field.shape[1] // CF, CF, field.shape[2] // CF, CF)
    return jnp.mean(blocks, axis=(2, 4))


def prolong(field):
    return jnp.repeat(jnp.repeat(field, CF, axis=1), CF, axis=2)


def reference(c_state):
    coarse_courant = COURANT * FSTEPS / CF
    coarse_diffusion = DIFFUSION * FSTEPS / (CF * CF)

    def fine_run(field):
        for section_index in range(FSTEPS):
            field = advance(wrap_rows(field), COURANT, DIFFUSION)
        return field

    def coarse(field):
        return advance(wrap_rows(field), coarse_courant, coarse_diffusion)

    fine_end = lax.map(fine_run, c_state)
    start_coarse = jax.vmap(restrict)(c_state)
    end_coarse = jax.vmap(restrict)(fine_end)
    defect = end_coarse - jax.vmap(coarse)(start_coarse)

    def chain_step(carry, defect_term):
        advanced = coarse(carry) + defect_term
        return advanced, advanced

    unused, coarse_path = lax.scan(chain_step, start_coarse[0], defect)
    return fine_end + jax.vmap(prolong)(coarse_path - end_coarse)
```

```python
import functools

import jax
import jax.numpy as jnp
from jax import lax
from jax.experimental import pallas as pl
from jax.experimental.pallas import tpu as pltpu
from jax.sharding import PartitionSpec as P

FSTEPS = 4
CF = 4
COURANT = 0.06
DIFFUSION = 0.04
COARSE_COURANT = COURANT * FSTEPS / CF
COARSE_DIFFUSION = DIFFUSION * FSTEPS / (CF * CF)
EXT = 1
HALO = FSTEPS + CF * EXT
LANES = 128
VMEM = pl.BlockSpec(memory_space=pltpu.VMEM)
HIGHEST = lax.Precision.HIGHEST


def shifted(field, amount, axis):
    return pltpu.roll(field, amount % field.shape[axis], axis)


def advance(fields, courant, diffusion, pitch):
    u, v = fields
    along_u, along_v = courant * u, courant * v
    above = jnp.maximum(along_u, 0.0) + diffusion
    below = above - along_u
    left = jnp.maximum(along_v, 0.0) + diffusion
    right = left - along_v
    center = 1.0 - ((above + below) + (left + right))
    return [
        center * q
        + (above * shifted(q, pitch, 0) + below * shifted(q, -pitch, 0))
        + (left * shifted(q, 1, 1) + right * shifted(q, -1, 1))
        for q in fields
    ]


def column_means(field):
    fine = CF * LANES
    rows = lax.broadcasted_iota(jnp.int32, (fine, LANES), 0)
    cols = lax.broadcasted_iota(jnp.int32, (fine, LANES), 1)
    weights = jnp.where(rows // CF == cols, 1.0 / (CF * CF), 0.0).astype(jnp.float32)
    pieces = [field[:, at : at + fine] for at in range(0, field.shape[1], fine)]
    stacked = jnp.concatenate(pieces, axis=0)
    sums = jnp.dot(stacked, weights, precision=HIGHEST, preferred_element_type=jnp.float32)
    count = field.shape[0]
    return jnp.concatenate([sums[i * count : (i + 1) * count] for i in range(len(pieces))], axis=1)


def group_rows(field):
    total, step = field, 1
    while step < CF:
        total = total + shifted(total, -step, 0)
        step *= 2
    return total


def spread(tile):
    fine = CF * LANES
    rows = lax.broadcasted_iota(jnp.int32, (LANES, fine), 0)
    cols = lax.broadcasted_iota(jnp.int32, (LANES, fine), 1)
    weights = jnp.where(cols // CF == rows, 1.0, 0.0).astype(jnp.float32)
    pieces = [tile[:, at : at + LANES] for at in range(0, tile.shape[1], LANES)]
    stacked = jnp.concatenate(pieces, axis=0)
    wide = jnp.dot(stacked, weights, precision=HIGHEST, preferred_element_type=jnp.float32)
    count = tile.shape[0]
    return jnp.concatenate([wide[i * count : (i + 1) * count] for i in range(len(pieces))], axis=1)


def repeat_rows(field, first, pitch, count):
    cols = field.shape[1]
    return jnp.concatenate(
        [
            jnp.broadcast_to(field[first + m * pitch : first + m * pitch + 1], (CF, cols))
            for m in range(count // CF)
        ],
        axis=0,
    )


def fine_kernel(near_ref, own_ref, far_ref, sent_ref, base_ref):
    rows = own_ref.shape[1]
    odd = lax.axis_index("space") % 2 == 1
    first_group = lax.axis_index("tm") == 0
    fields = []
    for q in range(2):
        near, far = near_ref[q], far_ref[q]
        low, high = jnp.where(odd, near, far), jnp.where(odd, far, near)
        fields.append(jnp.concatenate([low, own_ref[q], high], axis=0))
    start = [group_rows(column_means(q)) for q in fields]
    for _ in range(FSTEPS):
        fields = advance(fields, COURANT, DIFFUSION, 1)
    end = [group_rows(column_means(q)) for q in fields]
    coarse = advance(start, COARSE_COURANT, COARSE_DIFFUSION, CF)
    for q in range(2):
        defect = end[q] - coarse[q]
        sent = jnp.where(first_group, coarse[q] + defect, defect)
        for m in range(rows // CF + 2 * EXT):
            at = HALO - CF * EXT + CF * m
            sent_ref[q, m : m + 1, :] = sent[at : at + 1]
        lifted = spread(repeat_rows(end[q], HALO, CF, rows))
        base_ref[q] = fields[q][HALO : HALO + rows] - lifted


def window_kernel(depth, own_ref, near_ref, far_ref, *rest):
    others, window_ref = rest[:-1], rest[-1]
    odd = lax.axis_index("space") % 2 == 1
    inner = own_ref.shape[1] - 2 * EXT
    for q in range(2):
        near, far = near_ref[q], far_ref[q]
        low, high = [jnp.where(odd, near, far)], [jnp.where(odd, far, near)]
        low += [others[2 * d][q] for d in range(depth - 1)]
        high += [others[2 * d + 1][q] for d in range(depth - 1)]
        parts = [low[-1][: EXT + inner]]
        parts += [part[EXT : EXT + inner] for part in reversed(low[:-1])]
        parts += [own_ref[q, EXT : EXT + inner]]
        parts += [part[EXT : EXT + inner] for part in high[:-1]]
        parts += [high[-1][EXT:]]
        window_ref[q] = jnp.concatenate(parts, axis=0)


def chain_kernel(base_ref, *rest):
    held, out_ref = rest[:-1], rest[-1]
    groups = len(held)
    group = lax.axis_index("tm")

    def of(index):
        wanted = lax.bitwise_xor(group, index)
        picked = [held[0][q] for q in range(2)]
        for k in range(1, groups):
            picked = [jnp.where(wanted == k, held[k][q], picked[q]) for q in range(2)]
        return picked

    path = of(0)
    for index in range(1, groups):
        term = of(index)
        after = advance(path, COARSE_COURANT, COARSE_DIFFUSION, 1)
        path = [jnp.where(index <= group, after[q] + term[q], path[q]) for q in range(2)]
    rows = base_ref.shape[1]
    first = (path[0].shape[0] - rows // CF) // 2
    for q in range(2):
        out_ref[q] = base_ref[q] + spread(repeat_rows(path[q], first, 1, rows))


def call(kernel, shapes, *operands):
    return pl.pallas_call(
        kernel,
        out_shape=[jax.ShapeDtypeStruct(shape, jnp.float32) for shape in shapes],
        in_specs=[VMEM] * len(operands),
        out_specs=[VMEM] * len(shapes),
        compiler_params=pltpu.CompilerParams(vmem_limit_bytes=16 * 1024 * 1024),
    )(*operands)


def exchange(near_block, far_block):
    count = lax.axis_size("space")
    far = [(i, (i + 1 if i % 2 else i - 1) % count) for i in range(count)]
    near = [(i, i ^ 1) for i in range(count)]
    from_far = lax.ppermute(far_block, "space", far)
    from_near = lax.ppermute(near_block, "space", near)
    return from_near, from_far


def body(c_state):
    own = c_state[0]
    rows, cols = own.shape[1:]
    count, groups = lax.axis_size("space"), lax.axis_size("tm")
    assert rows == HALO and count % 2 == 0 and groups & (groups - 1) == 0
    inner, wide = rows // CF, cols // CF
    near, far = exchange(own, own)
    sent, base = call(fine_kernel, [(2, inner + 2 * EXT, wide), own.shape], near, own, far)
    reach = groups - 1
    depth = -(-(reach - EXT) // inner)
    pieces = [sent, *exchange(sent, sent)]
    for d in range(2, depth + 1):
        for sign in (1, -1):
            pairs = [(i, (i + sign * d) % count) for i in range(count)]
            pieces.append(lax.ppermute(sent, "space", pairs))
    (window,) = call(
        functools.partial(window_kernel, depth), [(2, inner * (2 * depth + 1) + 2 * EXT, wide)], *pieces
    )
    held = [window] + [None] * (groups - 1)
    for k in range(groups - 1, 0, -1):
        held[k] = lax.ppermute(window, "tm", [(i, i ^ k) for i in range(groups)])
    (after,) = call(chain_kernel, [own.shape], base, *held)
    return after[None]


def solution(mesh):
    placed = (P("tm", None, "space", None),)
    return jax.shard_map(
        body, mesh=mesh, in_specs=placed, out_specs=P("tm", None, "space", None), check_vma=False
    )
```

```python
import functools

import jax
import jax.numpy as jnp
from jax import lax
from jax.experimental import pallas as pl
from jax.experimental.pallas import tpu as pltpu
from jax.sharding import PartitionSpec as P

FSTEPS = 4
CF = 4
COURANT = 0.06
DIFFUSION = 0.04
COARSE_COURANT = COURANT * FSTEPS / CF
COARSE_DIFFUSION = DIFFUSION * FSTEPS / (CF * CF)
EXT = 1
HALO = FSTEPS + CF * EXT
LANES = 128
VMEM = pl.BlockSpec(memory_space=pltpu.VMEM)
ROWS = 8


def shifted(field, amount, axis):
    return pltpu.roll(field, amount % field.shape[axis], axis)


def advance(fields, courant, diffusion, pitch):
    u, v = fields
    along_u, along_v = courant * u, courant * v
    above = jnp.maximum(along_u, 0.0) + diffusion
    below = above - along_u
    left = jnp.maximum(along_v, 0.0) + diffusion
    right = left - along_v
    center = 1.0 - ((above + below) + (left + right))
    return [
        center * q
        + (above * shifted(q, pitch, 0) + below * shifted(q, -pitch, 0))
        + (left * shifted(q, 1, 1) + right * shifted(q, -1, 1))
        for q in fields
    ]


def exact_dot(field, weights):
    total = None
    for part in range(3):
        piece = field.astype(jnp.bfloat16)
        if part < 2:
            field = field - piece.astype(jnp.float32)
        product = jnp.dot(piece, weights, preferred_element_type=jnp.float32)
        total = product if total is None else total + product
    return total


def block_weights(shape, value):
    long = 0 if shape[0] > shape[1] else 1
    at = lax.broadcasted_iota(jnp.int32, shape, long)
    to = lax.broadcasted_iota(jnp.int32, shape, 1 - long)
    return jnp.where(at // CF == to, value, 0.0).astype(jnp.bfloat16)


def by_pieces(field, weights):
    width, count = weights.shape[0], field.shape[0]
    pieces = [field[:, at : at + width] for at in range(0, field.shape[1], width)]
    done = exact_dot(jnp.concatenate(pieces, axis=0), weights)
    return jnp.concatenate([done[i * count : (i + 1) * count] for i in range(len(pieces))], axis=1)


def packed_sums(tiles):
    packed = None
    for i, tile in enumerate(tiles):
        total = tile + shifted(tile, -1, 0)
        total = total + shifted(total, -2, 0)
        if packed is None:
            packed = total
        else:
            row = lax.broadcasted_iota(jnp.int32, tile.shape, 0)
            packed = jnp.where(row % CF == i, shifted(total, i, 0), packed)
    return packed


def sums_of(means, i):
    return [means[i : i + 1], means[CF + i : CF + i + 1]]


def repeat_rows(first, second):
    cols = first.shape[1]
    row = lax.broadcasted_iota(jnp.int32, (ROWS, cols), 0)
    return jnp.where(
        row < CF, jnp.broadcast_to(first, (ROWS, cols)), jnp.broadcast_to(second, (ROWS, cols))
    )


def near_kernel(
    near_ref, own_hbm, first_ref, second_ref, kept_ref, means_ref, gather_ref, spread_ref, own_ref, sem
):
    load = pltpu.make_async_copy(own_hbm, own_ref, sem)
    load.start()
    gather_ref[...] = block_weights(gather_ref.shape, 1.0 / (CF * CF))
    spread_ref[...] = block_weights(spread_ref.shape, 1.0)
    odd = lax.axis_index("space") % 2 == 1
    load.wait()
    fields = []
    for q in range(2):
        near, own = near_ref[q], own_ref[q]
        low, high = jnp.where(odd, near, own), jnp.where(odd, own, near)
        fields.append(jnp.concatenate([low, high], axis=0))
    near_sums = packed_sums([near_ref[0], near_ref[1], own_ref[0], own_ref[1]])
    for k in range(1, FSTEPS + 1):
        for q in range(2):
            own = jnp.where(odd, fields[q][ROWS:], fields[q][:ROWS])
            first_ref[k - 1, q] = pltpu.roll(own, jnp.where(odd, k, ROWS - k), 0)
            second_ref[k - 1, q] = pltpu.roll(own, jnp.where(odd, k + 1, ROWS - 1 - k), 0)
        fields = advance(fields, COURANT, DIFFUSION, 1)
    kept = [shifted(q, -CF, 0)[:ROWS] for q in fields]
    for q in range(2):
        kept_ref[q] = kept[q]
    end_sums = packed_sums(kept)
    both = by_pieces(jnp.concatenate([near_sums, end_sums], axis=0), gather_ref[...])
    means_ref[...] = both


def far_kernel(far_ref, first_ref, second_ref, means_ref, gather_ref, end_ref, sent_ref, ends_ref):
    odd = lax.axis_index("space") % 2 == 1
    first_group = lax.axis_index("tm") == 0
    sign = jnp.where(odd, 1.0, -1.0)
    turn = jnp.where(odd, 1, ROWS - 1)
    fields = [far_ref[0], far_ref[1]]
    starts = packed_sums(fields)
    row = lax.broadcasted_iota(jnp.int32, fields[0].shape, 0)
    edge = row == jnp.where(odd, 0, ROWS - 1)
    for k in range(FSTEPS):
        outer = fields
        fields = [jnp.where(edge, first_ref[k, q], pltpu.roll(outer[q], turn, 0)) for q in range(2)]
        inner = [jnp.where(edge, second_ref[k, q], pltpu.roll(fields[q], turn, 0)) for q in range(2)]
        along_u, along_v = (sign * COURANT) * fields[0], COURANT * fields[1]
        toward = jnp.maximum(along_u, 0.0) + DIFFUSION
        away = toward - along_u
        left = jnp.maximum(along_v, 0.0) + DIFFUSION
        right = left - along_v
        center = 1.0 - ((toward + away) + (left + right))
        fields = [
            center * fields[q]
            + (toward * inner[q] + away * outer[q])
            + (left * shifted(fields[q], 1, 1) + right * shifted(fields[q], -1, 1))
            for q in range(2)
        ]
    for q in range(2):
        end_ref[q] = fields[q]
    ends = packed_sums(fields)
    pack = jnp.where(row % CF < 2, ends, shifted(starts, 2, 0))
    far_means = by_pieces(pack, gather_ref[...])
    means = means_ref[...]
    near_means, near_ends = means[:ROWS], means[ROWS:]
    start, end = [], []
    for q in range(2):
        near, own, far = sums_of(near_means, q), sums_of(near_means, 2 + q), sums_of(far_means, 2 + q)
        this, that = sums_of(near_ends, q), sums_of(far_means, q)
        none = jnp.zeros_like(own[0])
        low = [jnp.where(odd, near[i], far[i]) for i in range(2)]
        high = [jnp.where(odd, far[i], near[i]) for i in range(2)]
        start.append(jnp.concatenate([*low, *own, *high, none, none], axis=0))
        low = [jnp.where(odd, this[i], that[i]) for i in range(2)]
        high = [jnp.where(odd, that[i], this[i]) for i in range(2)]
        end.append(jnp.concatenate([none, *low, *high, none, none, none], axis=0))
        ends_ref[q] = jnp.concatenate([low[1], high[0]], axis=0)
    coarse = advance(start, COARSE_COURANT, COARSE_DIFFUSION, 1)
    for q in range(2):
        defect = end[q] - coarse[q]
        sent = jnp.where(first_group, coarse[q] + defect, defect)
        sent_ref[q] = sent[EXT : EXT + 2 + 2 * EXT]


def window_kernel(depth, own_ref, near_ref, far_ref, *rest):
    others, window_ref = rest[:-1], rest[-1]
    odd = lax.axis_index("space") % 2 == 1
    inner = own_ref.shape[1] - 2 * EXT
    for q in range(2):
        near, far = near_ref[q], far_ref[q]
        low, high = [jnp.where(odd, near, far)], [jnp.where(odd, far, near)]
        low += [others[2 * d][q] for d in range(depth - 1)]
        high += [others[2 * d + 1][q] for d in range(depth - 1)]
        parts = [low[-1][: EXT + inner]]
        parts += [part[EXT : EXT + inner] for part in reversed(low[:-1])]
        parts += [own_ref[q, EXT : EXT + inner]]
        parts += [part[EXT : EXT + inner] for part in high[:-1]]
        parts += [high[-1][EXT:]]
        window_ref[q] = jnp.concatenate(parts, axis=0)


def chain_kernel(kept_ref, end_ref, ends_ref, spread_ref, *rest):
    held, out_ref = rest[:-1], rest[-1]
    groups = len(held)
    group = lax.axis_index("tm")

    def of(index):
        wanted = lax.bitwise_xor(group, index)
        picked = [held[0][q] for q in range(2)]
        for k in range(1, groups):
            picked = [jnp.where(wanted == k, held[k][q], picked[q]) for q in range(2)]
        return picked

    path = of(0)
    for index in range(1, groups):
        term = of(index)
        after = advance(path, COARSE_COURANT, COARSE_DIFFUSION, 1)
        path = [jnp.where(index <= group, after[q] + term[q], path[q]) for q in range(2)]
    first = (path[0].shape[0] - 2) // 2
    odd = lax.axis_index("space") % 2 == 1
    moves = []
    for q in range(2):
        move = path[q][first : first + 2] - ends_ref[q]
        moves.append(repeat_rows(move[:1], move[1:]))
    lifted = by_pieces(jnp.concatenate(moves, axis=0), spread_ref[...])
    for q in range(2):
        kept, end = kept_ref[q], end_ref[q]
        upper = lax.broadcasted_iota(jnp.int32, kept.shape, 0) >= CF
        own = shifted(jnp.where(upper == odd, kept, end), CF, 0)
        out_ref[q] = own + lifted[q * ROWS : (q + 1) * ROWS]


def call(kernel, shapes, operands, cost=0, hbm=(), scratch=()):
    where = [pl.BlockSpec(memory_space=pl.ANY) if i in hbm else VMEM for i in range(len(operands))]
    return pl.pallas_call(
        kernel,
        out_shape=[jax.ShapeDtypeStruct(shape, dtype) for shape, dtype in shapes],
        in_specs=where,
        out_specs=[VMEM] * len(shapes),
        scratch_shapes=scratch,
        cost_estimate=pl.CostEstimate(flops=cost, bytes_accessed=cost // 8, transcendentals=0),
        compiler_params=pltpu.CompilerParams(vmem_limit_bytes=16 * 1024 * 1024),
    )(*operands)


def exchange(near_block, far_block):
    count = lax.axis_size("space")
    far = [(i, (i + 1 if i % 2 else i - 1) % count) for i in range(count)]
    near = [(i, i ^ 1) for i in range(count)]
    from_far = lax.ppermute(far_block, "space", far)
    from_near = lax.ppermute(near_block, "space", near)
    return from_near, from_far


def body(c_state):
    own = c_state[0]
    rows, cols = own.shape[1:]
    count, groups = lax.axis_size("space"), lax.axis_size("tm")
    assert rows == HALO == ROWS and count % 2 == 0 and groups & (groups - 1) == 0
    full, half = jnp.float32, jnp.bfloat16
    inner, wide = rows // CF, cols // CF
    near, far = exchange(own, own)
    edges = ((FSTEPS, *own.shape), full)
    first, second, kept, means, gather, spread = call(
        near_kernel,
        [
            edges,
            edges,
            (own.shape, full),
            ((2 * ROWS, wide), full),
            ((CF * LANES, LANES), half),
            ((LANES, CF * LANES), half),
        ],
        (near, own),
        cost=8_000_000,
        hbm=(1,),
        scratch=[pltpu.VMEM(own.shape, full), pltpu.SemaphoreType.DMA],
    )
    end, sent, ends = call(
        far_kernel,
        [(own.shape, full), ((2, inner + 2 * EXT, wide), full), ((2, inner, wide), full)],
        (far, first, second, means, gather),
        cost=2_000_000,
    )
    reach = groups - 1
    depth = -(-(reach - EXT) // inner)
    pieces = [sent, *exchange(sent, sent)]
    for d in range(2, depth + 1):
        for sign in (1, -1):
            pairs = [(i, (i + sign * d) % count) for i in range(count)]
            pieces.append(lax.ppermute(sent, "space", pairs))
    (window,) = call(
        functools.partial(window_kernel, depth),
        [((2, inner * (2 * depth + 1) + 2 * EXT, wide), full)],
        pieces,
    )
    held = [window] + [None] * (groups - 1)
    for k in range(groups - 1, 0, -1):
        held[k] = lax.ppermute(window, "tm", [(i, i ^ k) for i in range(groups)])
    (after,) = call(chain_kernel, [(own.shape, full)], (kept, end, ends, spread, *held), cost=1_000_000)
    return after[None]


def solution(mesh):
    placed = (P("tm", None, "space", None),)
    return jax.shard_map(
        body, mesh=mesh, in_specs=placed, out_specs=P("tm", None, "space", None), check_vma=False
    )
```

```python
import functools

import jax
import jax.numpy as jnp
from jax import lax
from jax.experimental import pallas as pl
from jax.experimental.pallas import tpu as pltpu
from jax.sharding import PartitionSpec as P


FSTEPS = 4
CF = 4
COURANT = 0.06
DIFFUSION = 0.04
COARSE_COURANT = COURANT * FSTEPS / CF
COARSE_DIFFUSION = DIFFUSION * FSTEPS / (CF * CF)
EXT = 1
HALO = FSTEPS + CF * EXT
LANES = 128
VMEM = pl.BlockSpec(memory_space=pltpu.VMEM)
ROWS = 8


def shifted(field, amount, axis):
    return pltpu.roll(field, amount % field.shape[axis], axis)


def advance(fields, courant, diffusion, pitch):
    u, v = fields
    along_u, along_v = courant * u, courant * v
    above = jnp.maximum(along_u, 0.0) + diffusion
    below = above - along_u
    left = jnp.maximum(along_v, 0.0) + diffusion
    right = left - along_v
    center = 1.0 - ((above + below) + (left + right))
    return [
        center * q
        + (above * shifted(q, pitch, 0) + below * shifted(q, -pitch, 0))
        + (left * shifted(q, 1, 1) + right * shifted(q, -1, 1))
        for q in fields
    ]


def exact_dot(field, weights):
    total = None
    for part in range(3):
        piece = field.astype(jnp.bfloat16)
        if part < 2:
            field = field - piece.astype(jnp.float32)
        product = jnp.dot(piece, weights, preferred_element_type=jnp.float32)
        total = product if total is None else total + product
    return total


def block_weights(shape, value):
    long = 0 if shape[0] > shape[1] else 1
    at = lax.broadcasted_iota(jnp.int32, shape, long)
    to = lax.broadcasted_iota(jnp.int32, shape, 1 - long)
    return jnp.where(at // CF == to, value, 0.0).astype(jnp.bfloat16)


def by_pieces(field, weights):
    width, count = weights.shape[0], field.shape[0]
    pieces = [field[:, at : at + width] for at in range(0, field.shape[1], width)]
    done = exact_dot(jnp.concatenate(pieces, axis=0), weights)
    return jnp.concatenate([done[i * count : (i + 1) * count] for i in range(len(pieces))], axis=1)


def packed_sums(tiles):
    packed = None
    for i, tile in enumerate(tiles):
        total = tile + shifted(tile, -1, 0)
        total = total + shifted(total, -2, 0)
        if packed is None:
            packed = total
        else:
            row = lax.broadcasted_iota(jnp.int32, tile.shape, 0)
            packed = jnp.where(row % CF == i, shifted(total, i, 0), packed)
    return packed


def sums_of(means, i):
    return [means[i : i + 1], means[CF + i : CF + i + 1]]


def repeat_rows(first, second):
    cols = first.shape[1]
    row = lax.broadcasted_iota(jnp.int32, (ROWS, cols), 0)
    return jnp.where(
        row < CF, jnp.broadcast_to(first, (ROWS, cols)), jnp.broadcast_to(second, (ROWS, cols))
    )


def ready_kernel(own_hbm, own_ref, sums_ref, gather_ref, spread_ref, sem):
    load = pltpu.make_async_copy(own_hbm, own_ref, sem)
    load.start()
    gather_ref[...] = block_weights(gather_ref.shape, 1.0 / (CF * CF))
    spread_ref[...] = block_weights(spread_ref.shape, 1.0)
    load.wait()
    sums_ref[...] = packed_sums([own_ref[0], own_ref[1]])


def near_kernel(
    near_ref, own_ref, sums_ref, gather_ref, first_ref, second_ref, kept_ref, means_ref
):
    odd = lax.axis_index("space") % 2 == 1
    fields = []
    for q in range(2):
        near, own = near_ref[q], own_ref[q]
        low, high = jnp.where(odd, near, own), jnp.where(odd, own, near)
        fields.append(jnp.concatenate([low, high], axis=0))
    near_sums = packed_sums([near_ref[0], near_ref[1]])
    row = lax.broadcasted_iota(jnp.int32, near_sums.shape, 0)
    near_sums = jnp.where(row % CF < 2, near_sums, shifted(sums_ref[...], 2, 0))
    for k in range(1, FSTEPS + 1):
        for q in range(2):
            own = jnp.where(odd, fields[q][ROWS:], fields[q][:ROWS])
            first_ref[k - 1, q] = pltpu.roll(own, jnp.where(odd, k, ROWS - k), 0)
            second_ref[k - 1, q] = pltpu.roll(own, jnp.where(odd, k + 1, ROWS - 1 - k), 0)
        fields = advance(fields, COURANT, DIFFUSION, 1)
    kept = [shifted(q, -CF, 0)[:ROWS] for q in fields]
    for q in range(2):
        kept_ref[q] = kept[q]
    end_sums = packed_sums(kept)
    both = by_pieces(jnp.concatenate([near_sums, end_sums], axis=0), gather_ref[...])
    means_ref[...] = both


def far_kernel(far_ref, first_ref, second_ref, means_ref, gather_ref, end_ref, sent_ref, ends_ref):
    odd = lax.axis_index("space") % 2 == 1
    first_group = lax.axis_index("tm") == 0
    sign = jnp.where(odd, 1.0, -1.0)
    turn = jnp.where(odd, 1, ROWS - 1)
    fields = [far_ref[0], far_ref[1]]
    starts = packed_sums(fields)
    row = lax.broadcasted_iota(jnp.int32, fields[0].shape, 0)
    edge = row == jnp.where(odd, 0, ROWS - 1)
    for k in range(FSTEPS):
        outer = fields
        fields = [jnp.where(edge, first_ref[k, q], pltpu.roll(outer[q], turn, 0)) for q in range(2)]
        inner = [jnp.where(edge, second_ref[k, q], pltpu.roll(fields[q], turn, 0)) for q in range(2)]
        along_u, along_v = (sign * COURANT) * fields[0], COURANT * fields[1]
        toward = jnp.maximum(along_u, 0.0) + DIFFUSION
        away = toward - along_u
        left = jnp.maximum(along_v, 0.0) + DIFFUSION
        right = left - along_v
        center = 1.0 - ((toward + away) + (left + right))
        fields = [
            center * fields[q]
            + (toward * inner[q] + away * outer[q])
            + (left * shifted(fields[q], 1, 1) + right * shifted(fields[q], -1, 1))
            for q in range(2)
        ]
    for q in range(2):
        end_ref[q] = fields[q]
    ends = packed_sums(fields)
    pack = jnp.where(row % CF < 2, ends, shifted(starts, 2, 0))
    far_means = by_pieces(pack, gather_ref[...])
    means = means_ref[...]
    near_means, near_ends = means[:ROWS], means[ROWS:]
    start, end = [], []
    for q in range(2):
        near, own, far = sums_of(near_means, q), sums_of(near_means, 2 + q), sums_of(far_means, 2 + q)
        this, that = sums_of(near_ends, q), sums_of(far_means, q)
        none = jnp.zeros_like(own[0])
        low = [jnp.where(odd, near[i], far[i]) for i in range(2)]
        high = [jnp.where(odd, far[i], near[i]) for i in range(2)]
        start.append(jnp.concatenate([*low, *own, *high, none, none], axis=0))
        low = [jnp.where(odd, this[i], that[i]) for i in range(2)]
        high = [jnp.where(odd, that[i], this[i]) for i in range(2)]
        end.append(jnp.concatenate([none, *low, *high, none, none, none], axis=0))
        ends_ref[q] = jnp.concatenate([low[1], high[0]], axis=0)
    coarse = advance(start, COARSE_COURANT, COARSE_DIFFUSION, 1)
    for q in range(2):
        defect = end[q] - coarse[q]
        sent = jnp.where(first_group, coarse[q] + defect, defect)
        sent_ref[q] = sent[EXT : EXT + 2 + 2 * EXT]


def window_kernel(depth, own_ref, near_ref, far_ref, *rest):
    others, window_ref = rest[:-1], rest[-1]
    odd = lax.axis_index("space") % 2 == 1
    inner = own_ref.shape[1] - 2 * EXT
    for q in range(2):
        near, far = near_ref[q], far_ref[q]
        low, high = [jnp.where(odd, near, far)], [jnp.where(odd, far, near)]
        low += [others[2 * d][q] for d in range(depth - 1)]
        high += [others[2 * d + 1][q] for d in range(depth - 1)]
        parts = [low[-1][: EXT + inner]]
        parts += [part[EXT : EXT + inner] for part in reversed(low[:-1])]
        parts += [own_ref[q, EXT : EXT + inner]]
        parts += [part[EXT : EXT + inner] for part in high[:-1]]
        parts += [high[-1][EXT:]]
        window_ref[q] = jnp.concatenate(parts, axis=0)


def chain_kernel(kept_ref, end_ref, ends_ref, spread_ref, *rest):
    held, out_ref = rest[:-1], rest[-1]
    groups = len(held)
    group = lax.axis_index("tm")
    reach = max(ref.shape[1] for ref in held)

    def placed(ref, q):
        term = ref[q]
        spare = (reach - term.shape[0]) // 2
        if spare:
            none = jnp.zeros((spare, term.shape[1]), jnp.float32)
            term = jnp.concatenate([none, term, none], axis=0)
        return term

    terms = [[placed(ref, q) for q in range(2)] for ref in held]

    def of(index):
        picked = terms[0]
        for k in range(1, groups - index):
            picked = [jnp.where(group == index + k, terms[k][q], picked[q]) for q in range(2)]
        return picked

    path = of(0)
    for index in range(1, groups):
        term = of(index)
        after = advance(path, COARSE_COURANT, COARSE_DIFFUSION, 1)
        path = [jnp.where(index <= group, after[q] + term[q], path[q]) for q in range(2)]
    first = (path[0].shape[0] - 2) // 2
    odd = lax.axis_index("space") % 2 == 1
    moves = []
    for q in range(2):
        move = path[q][first : first + 2] - ends_ref[q]
        moves.append(repeat_rows(move[:1], move[1:]))
    lifted = by_pieces(jnp.concatenate(moves, axis=0), spread_ref[...])
    for q in range(2):
        kept, end = kept_ref[q], end_ref[q]
        upper = lax.broadcasted_iota(jnp.int32, kept.shape, 0) >= CF
        own = shifted(jnp.where(upper == odd, kept, end), CF, 0)
        out_ref[q] = own + lifted[q * ROWS : (q + 1) * ROWS]


def call(kernel, shapes, operands, cost=0, hbm=(), scratch=()):
    where = [pl.BlockSpec(memory_space=pl.ANY) if i in hbm else VMEM for i in range(len(operands))]
    return pl.pallas_call(
        kernel,
        out_shape=[jax.ShapeDtypeStruct(shape, dtype) for shape, dtype in shapes],
        in_specs=where,
        out_specs=[VMEM] * len(shapes),
        scratch_shapes=scratch,
        cost_estimate=pl.CostEstimate(flops=cost, bytes_accessed=cost // 8, transcendentals=0),
        compiler_params=pltpu.CompilerParams(vmem_limit_bytes=16 * 1024 * 1024),
    )(*operands)


def exchange(block):
    count = lax.axis_size("space")
    far = [(i, (i + 1 if i % 2 else i - 1) % count) for i in range(count)]
    near = [(i, i ^ 1) for i in range(count)]
    from_far = lax.ppermute(block, "space", far)
    from_near = lax.ppermute(block, "space", near)
    return from_near, from_far


def step(c_state):
    own = c_state[0]
    rows, cols = own.shape[1:]
    count, groups = lax.axis_size("space"), lax.axis_size("tm")
    assert rows == HALO == ROWS and count % 2 == 0
    full, half = jnp.float32, jnp.bfloat16
    inner, wide = rows // CF, cols // CF
    near, far = exchange(own)
    own_here, own_sums, gather, spread = call(
        ready_kernel,
        [
            (own.shape, full),
            ((ROWS, cols), full),
            ((CF * LANES, LANES), half),
            ((LANES, CF * LANES), half),
        ],
        (own,),
        cost=4_000_000,
        hbm=(0,),
        scratch=[pltpu.SemaphoreType.DMA],
    )
    edges = ((FSTEPS, *own.shape), full)
    first, second, kept, means = call(
        near_kernel,
        [edges, edges, (own.shape, full), ((2 * ROWS, wide), full)],
        (near, own_here, own_sums, gather),
        cost=8_000_000,
    )
    end, sent, ends = call(
        far_kernel,
        [(own.shape, full), ((2, inner + 2 * EXT, wide), full), ((2, inner, wide), full)],
        (far, first, second, means, gather),
        cost=2_000_000,
    )
    reach = groups - 1
    depth = -(-(reach - EXT) // inner)
    pieces = [sent, *exchange(sent)]
    for d in range(2, depth + 1):
        for sign in (1, -1):
            pairs = [(i, (i + sign * d) % count) for i in range(count)]
            pieces.append(lax.ppermute(sent, "space", pairs))
    (window,) = call(
        functools.partial(window_kernel, depth),
        [((2, inner * (2 * depth + 1) + 2 * EXT, wide), full)],
        pieces,
    )
    held = [sent]
    for k in range(1, groups):
        pairs = [(i, (i + k) % groups) for i in range(groups)]
        held.append(lax.ppermute(sent if k <= EXT else window, "tm", pairs))
    (after,) = call(chain_kernel, [(own.shape, full)], (kept, end, ends, spread, *held), cost=1_000_000)
    return after[None]


def solution(mesh):
    placed = (P("tm", None, "space", None),)
    return jax.shard_map(
        step, mesh=mesh, in_specs=placed, out_specs=P("tm", None, "space", None), check_vma=False
    )
```

```python
import functools

import jax
import jax.numpy as jnp
from jax import lax
from jax.experimental import pallas as pl
from jax.experimental.pallas import tpu as pltpu
from jax.sharding import PartitionSpec as P


FSTEPS = 4
CF = 4
COURANT = 0.06
DIFFUSION = 0.04
COARSE_COURANT = COURANT * FSTEPS / CF
COARSE_DIFFUSION = DIFFUSION * FSTEPS / (CF * CF)
EXT = 1
HALO = FSTEPS + CF * EXT
LANES = 128
VMEM = pl.BlockSpec(memory_space=pltpu.VMEM)
ROWS = 8


def shifted(field, amount, axis):
    return pltpu.roll(field, amount % field.shape[axis], axis)


def advance(fields, courant, diffusion, pitch):
    u, v = fields
    along_u, along_v = courant * u, courant * v
    above = jnp.maximum(along_u, 0.0) + diffusion
    below = above - along_u
    left = jnp.maximum(along_v, 0.0) + diffusion
    right = left - along_v
    center = 1.0 - ((above + below) + (left + right))
    return [
        center * q
        + (above * shifted(q, pitch, 0) + below * shifted(q, -pitch, 0))
        + (left * shifted(q, 1, 1) + right * shifted(q, -1, 1))
        for q in fields
    ]


def exact_dot(field, weights):
    total = None
    for part in range(3):
        piece = field.astype(jnp.bfloat16)
        if part < 2:
            field = field - piece.astype(jnp.float32)
        product = jnp.dot(piece, weights, preferred_element_type=jnp.float32)
        total = product if total is None else total + product
    return total


def block_weights(shape, value):
    long = 0 if shape[0] > shape[1] else 1
    at = lax.broadcasted_iota(jnp.int32, shape, long)
    to = lax.broadcasted_iota(jnp.int32, shape, 1 - long)
    return jnp.where(at // CF == to, value, 0.0).astype(jnp.bfloat16)


def by_pieces(field, weights):
    width, count = weights.shape[0], field.shape[0]
    pieces = [field[:, at : at + width] for at in range(0, field.shape[1], width)]
    done = exact_dot(jnp.concatenate(pieces, axis=0), weights)
    return jnp.concatenate([done[i * count : (i + 1) * count] for i in range(len(pieces))], axis=1)


def packed_sums(tiles):
    packed = None
    for i, tile in enumerate(tiles):
        total = tile + shifted(tile, -1, 0)
        total = total + shifted(total, -2, 0)
        if packed is None:
            packed = total
        else:
            row = lax.broadcasted_iota(jnp.int32, tile.shape, 0)
            packed = jnp.where(row % CF == i, shifted(total, i, 0), packed)
    return packed


def sums_of(means, i):
    return [means[i : i + 1], means[CF + i : CF + i + 1]]


def repeat_rows(first, second):
    cols = first.shape[1]
    row = lax.broadcasted_iota(jnp.int32, (ROWS, cols), 0)
    return jnp.where(
        row < CF, jnp.broadcast_to(first, (ROWS, cols)), jnp.broadcast_to(second, (ROWS, cols))
    )


def ready_kernel(own_hbm, own_ref, sums_ref, gather_ref, spread_ref, sem):
    load = pltpu.make_async_copy(own_hbm, own_ref, sem)
    load.start()
    gather_ref[...] = block_weights(gather_ref.shape, 1.0 / (CF * CF))
    spread_ref[...] = block_weights(spread_ref.shape, 1.0)
    load.wait()
    sums_ref[...] = packed_sums([own_ref[0], own_ref[1]])


def near_kernel(
    near_ref, own_ref, sums_ref, gather_ref, first_ref, second_ref, kept_ref, means_ref
):
    odd = lax.axis_index("space") % 2 == 1
    fields = []
    for q in range(2):
        near, own = near_ref[q], own_ref[q]
        low, high = jnp.where(odd, near, own), jnp.where(odd, own, near)
        fields.append(jnp.concatenate([low, high], axis=0))
    near_sums = packed_sums([near_ref[0], near_ref[1]])
    row = lax.broadcasted_iota(jnp.int32, near_sums.shape, 0)
    near_sums = jnp.where(row % CF < 2, near_sums, shifted(sums_ref[...], 2, 0))
    for k in range(1, FSTEPS + 1):
        for q in range(2):
            own = jnp.where(odd, fields[q][ROWS:], fields[q][:ROWS])
            first_ref[k - 1, q] = pltpu.roll(own, jnp.where(odd, k, ROWS - k), 0)
            second_ref[k - 1, q] = pltpu.roll(own, jnp.where(odd, k + 1, ROWS - 1 - k), 0)
        fields = advance(fields, COURANT, DIFFUSION, 1)
    kept = [shifted(q, -CF, 0)[:ROWS] for q in fields]
    for q in range(2):
        kept_ref[q] = kept[q]
    end_sums = packed_sums(kept)
    both = by_pieces(jnp.concatenate([near_sums, end_sums], axis=0), gather_ref[...])
    means_ref[...] = both


def far_kernel(far_ref, first_ref, second_ref, means_ref, gather_ref, end_ref, sent_ref, ends_ref):
    odd = lax.axis_index("space") % 2 == 1
    first_group = lax.axis_index("tm") == 0
    sign = jnp.where(odd, 1.0, -1.0)
    turn = jnp.where(odd, 1, ROWS - 1)
    fields = [far_ref[0], far_ref[1]]
    starts = packed_sums(fields)
    row = lax.broadcasted_iota(jnp.int32, fields[0].shape, 0)
    edge = row == jnp.where(odd, 0, ROWS - 1)
    for k in range(FSTEPS):
        outer = fields
        fields = [jnp.where(edge, first_ref[k, q], pltpu.roll(outer[q], turn, 0)) for q in range(2)]
        inner = [jnp.where(edge, second_ref[k, q], pltpu.roll(fields[q], turn, 0)) for q in range(2)]
        along_u, along_v = (sign * COURANT) * fields[0], COURANT * fields[1]
        toward = jnp.maximum(along_u, 0.0) + DIFFUSION
        away = toward - along_u
        left = jnp.maximum(along_v, 0.0) + DIFFUSION
        right = left - along_v
        center = 1.0 - ((toward + away) + (left + right))
        fields = [
            center * fields[q]
            + (toward * inner[q] + away * outer[q])
            + (left * shifted(fields[q], 1, 1) + right * shifted(fields[q], -1, 1))
            for q in range(2)
        ]
    for q in range(2):
        end_ref[q] = fields[q]
    ends = packed_sums(fields)
    pack = jnp.where(row % CF < 2, ends, shifted(starts, 2, 0))
    far_means = by_pieces(pack, gather_ref[...])
    means = means_ref[...]
    near_means, near_ends = means[:ROWS], means[ROWS:]
    start, end = [], []
    for q in range(2):
        near, own, far = sums_of(near_means, q), sums_of(near_means, 2 + q), sums_of(far_means, 2 + q)
        this, that = sums_of(near_ends, q), sums_of(far_means, q)
        none = jnp.zeros_like(own[0])
        low = [jnp.where(odd, near[i], far[i]) for i in range(2)]
        high = [jnp.where(odd, far[i], near[i]) for i in range(2)]
        start.append(jnp.concatenate([*low, *own, *high, none, none], axis=0))
        low = [jnp.where(odd, this[i], that[i]) for i in range(2)]
        high = [jnp.where(odd, that[i], this[i]) for i in range(2)]
        end.append(jnp.concatenate([none, *low, *high, none, none, none], axis=0))
        ends_ref[q] = jnp.concatenate([low[1], high[0]], axis=0)
    coarse = advance(start, COARSE_COURANT, COARSE_DIFFUSION, 1)
    for q in range(2):
        defect = end[q] - coarse[q]
        sent = jnp.where(first_group, coarse[q] + defect, defect)
        sent_ref[q] = sent[EXT : EXT + 2 + 2 * EXT]


def window_kernel(depth, own_ref, near_ref, far_ref, *rest):
    others, window_ref = rest[:-1], rest[-1]
    odd = lax.axis_index("space") % 2 == 1
    inner = own_ref.shape[1] - 2 * EXT
    for q in range(2):
        near, far = near_ref[q], far_ref[q]
        low, high = [jnp.where(odd, near, far)], [jnp.where(odd, far, near)]
        low += [others[2 * d][q] for d in range(depth - 1)]
        high += [others[2 * d + 1][q] for d in range(depth - 1)]
        parts = [low[-1][: EXT + inner]]
        parts += [part[EXT : EXT + inner] for part in reversed(low[:-1])]
        parts += [own_ref[q, EXT : EXT + inner]]
        parts += [part[EXT : EXT + inner] for part in high[:-1]]
        parts += [high[-1][EXT:]]
        window_ref[q] = jnp.concatenate(parts, axis=0)


def chain_kernel(kept_ref, end_ref, ends_ref, spread_ref, *rest):
    held, out_ref = rest[:-1], rest[-1]
    groups = len(held)
    group = lax.axis_index("tm")
    reach = max(ref.shape[1] for ref in held)

    def placed(ref, q):
        term = ref[q]
        spare = (reach - term.shape[0]) // 2
        if spare:
            none = jnp.zeros((spare, term.shape[1]), jnp.float32)
            term = jnp.concatenate([none, term, none], axis=0)
        return term

    terms = [[placed(ref, q) for q in range(2)] for ref in held]

    def of(index):
        picked = terms[0]
        for k in range(1, groups - index):
            picked = [jnp.where(group == index + k, terms[k][q], picked[q]) for q in range(2)]
        return picked

    path = of(0)
    for index in range(1, groups):
        term = of(index)
        after = advance(path, COARSE_COURANT, COARSE_DIFFUSION, 1)
        path = [jnp.where(index <= group, after[q] + term[q], path[q]) for q in range(2)]
    first = (path[0].shape[0] - 2) // 2
    odd = lax.axis_index("space") % 2 == 1
    moves = []
    for q in range(2):
        move = path[q][first : first + 2] - ends_ref[q]
        moves.append(repeat_rows(move[:1], move[1:]))
    lifted = by_pieces(jnp.concatenate(moves, axis=0), spread_ref[...])
    for q in range(2):
        kept, end = kept_ref[q], end_ref[q]
        upper = lax.broadcasted_iota(jnp.int32, kept.shape, 0) >= CF
        own = shifted(jnp.where(upper == odd, kept, end), CF, 0)
        out_ref[q] = own + lifted[q * ROWS : (q + 1) * ROWS]


def call(kernel, shapes, operands, cost=0, hbm=(), scratch=()):
    where = [pl.BlockSpec(memory_space=pl.ANY) if i in hbm else VMEM for i in range(len(operands))]
    return pl.pallas_call(
        kernel,
        out_shape=[jax.ShapeDtypeStruct(shape, dtype) for shape, dtype in shapes],
        in_specs=where,
        out_specs=[VMEM] * len(shapes),
        scratch_shapes=scratch,
        cost_estimate=pl.CostEstimate(flops=cost, bytes_accessed=cost // 8, transcendentals=0),
        compiler_params=pltpu.CompilerParams(vmem_limit_bytes=16 * 1024 * 1024),
    )(*operands)


def exchange(block, among):
    count, groups = lax.axis_size("space"), lax.axis_size("tm")
    far = [(i, (i + 1 if i % 2 else i - 1) % count) for i in range(count)]
    near = [(i, i ^ 1) for i in range(count)]
    mixed = [
        (t * count + a, t * count + b)
        for t in range(groups)
        for a, b in (far if t < among else near)
    ]
    from_far = lax.ppermute(block, ("tm", "space"), mixed)
    from_near = lax.ppermute(block, "space", near)
    return from_near, from_far


def forward(groups, distance):
    pairs = [(i, (i + distance) % groups) for i in range(groups)]
    if distance == 2 and groups > 2:
        pairs[-2:] = [(groups - 2, 1), (groups - 1, 0)]
    return pairs


def step(c_state):
    own = c_state[0]
    rows, cols = own.shape[1:]
    count, groups = lax.axis_size("space"), lax.axis_size("tm")
    assert rows == HALO == ROWS and count % 2 == 0
    full, half = jnp.float32, jnp.bfloat16
    inner, wide = rows // CF, cols // CF
    near, far = exchange(own, groups)
    own_here, own_sums, gather, spread = call(
        ready_kernel,
        [
            (own.shape, full),
            ((ROWS, cols), full),
            ((CF * LANES, LANES), half),
            ((LANES, CF * LANES), half),
        ],
        (own,),
        cost=4_000_000,
        hbm=(0,),
        scratch=[pltpu.SemaphoreType.DMA],
    )
    edges = ((FSTEPS, *own.shape), full)
    first, second, kept, means = call(
        near_kernel,
        [edges, edges, (own.shape, full), ((2 * ROWS, wide), full)],
        (near, own_here, own_sums, gather),
        cost=8_000_000,
    )
    end, sent, ends = call(
        far_kernel,
        [(own.shape, full), ((2, inner + 2 * EXT, wide), full), ((2, inner, wide), full)],
        (far, first, second, means, gather),
        cost=2_000_000,
    )
    reach = groups - 1
    depth = -(-(reach - EXT) // inner)
    pieces = [sent, *exchange(sent, groups - 1 - EXT)]
    for d in range(2, depth + 1):
        for sign in (1, -1):
            pairs = [(i, (i + sign * d) % count) for i in range(count)]
            pieces.append(lax.ppermute(sent, "space", pairs))
    (window,) = call(
        functools.partial(window_kernel, depth),
        [((2, inner * (2 * depth + 1) + 2 * EXT, wide), full)],
        pieces,
    )
    held = [sent]
    for k in range(1, groups):
        held.append(lax.ppermute(sent if k <= EXT else window, "tm", forward(groups, k)))
    (after,) = call(chain_kernel, [(own.shape, full)], (kept, end, ends, spread, *held), cost=1_000_000)
    return after[None]


def solution(mesh):
    placed = (P("tm", None, "space", None),)
    return jax.shard_map(
        step, mesh=mesh, in_specs=placed, out_specs=P("tm", None, "space", None), check_vma=False
    )
```

```python
import functools

import jax
import jax.numpy as jnp
from jax import lax
from jax.experimental import pallas as pl
from jax.experimental.pallas import tpu as pltpu
from jax.sharding import PartitionSpec as P


FSTEPS = 4
CF = 4
COURANT = 0.06
DIFFUSION = 0.04
COARSE_COURANT = COURANT * FSTEPS / CF
COARSE_DIFFUSION = DIFFUSION * FSTEPS / (CF * CF)
EXT = 1
HALO = FSTEPS + CF * EXT
LANES = 128
VMEM = pl.BlockSpec(memory_space=pltpu.VMEM)
ROWS = 8
OUT_PIECES = 2


def shifted(field, amount, axis):
    return pltpu.roll(field, amount % field.shape[axis], axis)


def advance(fields, courant, diffusion, pitch):
    u, v = fields
    along_u, along_v = courant * u, courant * v
    above = jnp.maximum(along_u, 0.0) + diffusion
    below = above - along_u
    left = jnp.maximum(along_v, 0.0) + diffusion
    right = left - along_v
    center = 1.0 - ((above + below) + (left + right))
    return [
        center * q
        + (above * shifted(q, pitch, 0) + below * shifted(q, -pitch, 0))
        + (left * shifted(q, 1, 1) + right * shifted(q, -1, 1))
        for q in fields
    ]


def exact_dot(field, weights):
    total = None
    for part in range(3):
        piece = field.astype(jnp.bfloat16)
        if part < 2:
            field = field - piece.astype(jnp.float32)
        product = jnp.dot(piece, weights, preferred_element_type=jnp.float32)
        total = product if total is None else total + product
    return total


def block_weights(shape, value):
    long = 0 if shape[0] > shape[1] else 1
    at = lax.broadcasted_iota(jnp.int32, shape, long)
    to = lax.broadcasted_iota(jnp.int32, shape, 1 - long)
    return jnp.where(at // CF == to, value, 0.0).astype(jnp.bfloat16)


def by_pieces(field, weights):
    width, count = weights.shape[0], field.shape[0]
    pieces = [field[:, at : at + width] for at in range(0, field.shape[1], width)]
    done = exact_dot(jnp.concatenate(pieces, axis=0), weights)
    return jnp.concatenate([done[i * count : (i + 1) * count] for i in range(len(pieces))], axis=1)


def packed_sums(tiles):
    packed = None
    for i, tile in enumerate(tiles):
        total = tile + shifted(tile, -1, 0)
        total = total + shifted(total, -2, 0)
        if packed is None:
            packed = total
        else:
            row = lax.broadcasted_iota(jnp.int32, tile.shape, 0)
            packed = jnp.where(row % CF == i, shifted(total, i, 0), packed)
    return packed


def sums_of(means, i):
    return [means[i : i + 1], means[CF + i : CF + i + 1]]


def repeat_rows(first, second):
    cols = first.shape[1]
    row = lax.broadcasted_iota(jnp.int32, (ROWS, cols), 0)
    return jnp.where(
        row < CF, jnp.broadcast_to(first, (ROWS, cols)), jnp.broadcast_to(second, (ROWS, cols))
    )


def ready_kernel(own_hbm, own_ref, sums_ref, gather_ref, spread_ref, sem):
    load = pltpu.make_async_copy(own_hbm, own_ref, sem)
    load.start()
    gather_ref[...] = block_weights(gather_ref.shape, 1.0 / (CF * CF))
    spread_ref[...] = block_weights(spread_ref.shape, 1.0)
    load.wait()
    sums_ref[...] = packed_sums([own_ref[0], own_ref[1]])


def near_kernel(
    near_ref, own_ref, sums_ref, gather_ref, first_ref, second_ref, kept_ref, means_ref
):
    odd = lax.axis_index("space") % 2 == 1
    fields = []
    for q in range(2):
        near, own = near_ref[q], own_ref[q]
        low, high = jnp.where(odd, near, own), jnp.where(odd, own, near)
        fields.append(jnp.concatenate([low, high], axis=0))
    near_sums = packed_sums([near_ref[0], near_ref[1]])
    row = lax.broadcasted_iota(jnp.int32, near_sums.shape, 0)
    near_sums = jnp.where(row % CF < 2, near_sums, shifted(sums_ref[...], 2, 0))
    for k in range(1, FSTEPS + 1):
        for q in range(2):
            own = jnp.where(odd, fields[q][ROWS:], fields[q][:ROWS])
            first_ref[k - 1, q] = pltpu.roll(own, jnp.where(odd, k, ROWS - k), 0)
            second_ref[k - 1, q] = pltpu.roll(own, jnp.where(odd, k + 1, ROWS - 1 - k), 0)
        fields = advance(fields, COURANT, DIFFUSION, 1)
    kept = [shifted(q, -CF, 0)[:ROWS] for q in fields]
    for q in range(2):
        kept_ref[q] = kept[q]
    end_sums = packed_sums(kept)
    both = by_pieces(jnp.concatenate([near_sums, end_sums], axis=0), gather_ref[...])
    means_ref[...] = both


def far_kernel(far_ref, first_ref, second_ref, means_ref, gather_ref, end_ref, sent_ref, ends_ref):
    odd = lax.axis_index("space") % 2 == 1
    first_group = lax.axis_index("tm") == 0
    sign = jnp.where(odd, 1.0, -1.0)
    turn = jnp.where(odd, 1, ROWS - 1)
    fields = [far_ref[0], far_ref[1]]
    starts = packed_sums(fields)
    row = lax.broadcasted_iota(jnp.int32, fields[0].shape, 0)
    edge = row == jnp.where(odd, 0, ROWS - 1)
    for k in range(FSTEPS):
        outer = fields
        fields = [jnp.where(edge, first_ref[k, q], pltpu.roll(outer[q], turn, 0)) for q in range(2)]
        inner = [jnp.where(edge, second_ref[k, q], pltpu.roll(fields[q], turn, 0)) for q in range(2)]
        along_u, along_v = (sign * COURANT) * fields[0], COURANT * fields[1]
        toward = jnp.maximum(along_u, 0.0) + DIFFUSION
        away = toward - along_u
        left = jnp.maximum(along_v, 0.0) + DIFFUSION
        right = left - along_v
        center = 1.0 - ((toward + away) + (left + right))
        fields = [
            center * fields[q]
            + (toward * inner[q] + away * outer[q])
            + (left * shifted(fields[q], 1, 1) + right * shifted(fields[q], -1, 1))
            for q in range(2)
        ]
    for q in range(2):
        end_ref[q] = fields[q]
    ends = packed_sums(fields)
    pack = jnp.where(row % CF < 2, ends, shifted(starts, 2, 0))
    far_means = by_pieces(pack, gather_ref[...])
    means = means_ref[...]
    near_means, near_ends = means[:ROWS], means[ROWS:]
    start, end = [], []
    for q in range(2):
        near, own, far = sums_of(near_means, q), sums_of(near_means, 2 + q), sums_of(far_means, 2 + q)
        this, that = sums_of(near_ends, q), sums_of(far_means, q)
        none = jnp.zeros_like(own[0])
        low = [jnp.where(odd, near[i], far[i]) for i in range(2)]
        high = [jnp.where(odd, far[i], near[i]) for i in range(2)]
        start.append(jnp.concatenate([*low, *own, *high, none, none], axis=0))
        low = [jnp.where(odd, this[i], that[i]) for i in range(2)]
        high = [jnp.where(odd, that[i], this[i]) for i in range(2)]
        end.append(jnp.concatenate([none, *low, *high, none, none, none], axis=0))
        ends_ref[q] = jnp.concatenate([low[1], high[0]], axis=0)
    coarse = advance(start, COARSE_COURANT, COARSE_DIFFUSION, 1)
    for q in range(2):
        defect = end[q] - coarse[q]
        sent = jnp.where(first_group, coarse[q] + defect, defect)
        sent_ref[q] = sent[EXT : EXT + 2 + 2 * EXT]


def window_kernel(depth, own_ref, near_ref, far_ref, *rest):
    others, window_ref = rest[:-1], rest[-1]
    odd = lax.axis_index("space") % 2 == 1
    inner = own_ref.shape[1] - 2 * EXT
    for q in range(2):
        near, far = near_ref[q], far_ref[q]
        low, high = [jnp.where(odd, near, far)], [jnp.where(odd, far, near)]
        low += [others[2 * d][q] for d in range(depth - 1)]
        high += [others[2 * d + 1][q] for d in range(depth - 1)]
        parts = [low[-1][: EXT + inner]]
        parts += [part[EXT : EXT + inner] for part in reversed(low[:-1])]
        parts += [own_ref[q, EXT : EXT + inner]]
        parts += [part[EXT : EXT + inner] for part in high[:-1]]
        parts += [high[-1][EXT:]]
        window_ref[q] = jnp.concatenate(parts, axis=0)


def corrected(group, groups, held, kept_ref, end_ref, ends_ref, spread_ref, out_hbm, stage_ref, sems):
    reach = max(ref.shape[1] for ref in held)

    def placed(ref, q):
        term = ref[q]
        spare = (reach - term.shape[0]) // 2
        if spare:
            none = jnp.zeros((spare, term.shape[1]), jnp.float32)
            term = jnp.concatenate([none, term, none], axis=0)
        return term

    terms = [[placed(ref, q) for q in range(2)] for ref in held]

    def of(index):
        if index == groups - 1:
            return terms[0]
        picked = terms[min(len(terms) - 1, groups - 1 - index)]
        for k in range(min(len(terms) - 1, groups - 1 - index) - 1, -1, -1):
            picked = [jnp.where(group == index + k, terms[k][q], picked[q]) for q in range(2)]
        return picked

    path = of(0)
    for index in range(1, groups):
        term = of(index)
        after = advance(path, COARSE_COURANT, COARSE_DIFFUSION, 1)
        path = [jnp.where(index <= group, after[q] + term[q], path[q]) for q in range(2)]
    first = (reach - 2) // 2
    odd = lax.axis_index("space") % 2 == 1
    moves, own = [], []
    for q in range(2):
        move = path[q][first : first + 2] - ends_ref[q]
        moves.append(repeat_rows(move[:1], move[1:]))
        upper = lax.broadcasted_iota(jnp.int32, kept_ref.shape[1:], 0) >= CF
        own.append(shifted(jnp.where(upper == odd, kept_ref[q], end_ref[q]), CF, 0))
    lifted = by_pieces(jnp.concatenate(moves, axis=0), spread_ref[...])
    copies = []
    width = out_hbm.shape[2] // OUT_PIECES
    for i in range(OUT_PIECES):
        cols = slice(i * width, (i + 1) * width)
        for q in range(2):
            stage_ref[q, :, cols] = own[q][:, cols] + lifted[q * ROWS : (q + 1) * ROWS, cols]
        copy = pltpu.make_async_copy(stage_ref.at[:, :, cols], out_hbm.at[:, :, cols], sems.at[i])
        copy.start()
        copies.append(copy)
    for copy in copies:
        copy.wait()


def early_kernel(among, kept_ref, end_ref, ends_ref, spread_ref, *rest):
    held, (out_hbm, stage_ref, sems) = rest[:-3], rest[-3:]
    group = lax.axis_index("tm")

    @pl.when(group < among)
    def _():
        corrected(
            group, among, held, kept_ref, end_ref, ends_ref, spread_ref, out_hbm, stage_ref, sems
        )


def late_kernel(groups, among, before_hbm, kept_ref, end_ref, ends_ref, spread_ref, *rest):
    held, (out_hbm, stage_ref, sems) = rest[:-3], rest[-3:]
    group = lax.axis_index("tm")

    @pl.when(group >= among)
    def _():
        corrected(
            group, groups, held, kept_ref, end_ref, ends_ref, spread_ref, out_hbm, stage_ref, sems
        )


def call(kernel, shapes, operands, cost=0, hbm=(), scratch=(), out=VMEM, alias=None):
    where = [pl.BlockSpec(memory_space=pl.ANY) if i in hbm else VMEM for i in range(len(operands))]
    return pl.pallas_call(
        kernel,
        out_shape=[jax.ShapeDtypeStruct(shape, dtype) for shape, dtype in shapes],
        in_specs=where,
        out_specs=[out] * len(shapes),
        input_output_aliases=alias or {},
        scratch_shapes=scratch,
        cost_estimate=pl.CostEstimate(flops=cost, bytes_accessed=cost // 8, transcendentals=0),
        compiler_params=pltpu.CompilerParams(vmem_limit_bytes=16 * 1024 * 1024),
    )(*operands)


def exchange(block, among):
    count, groups = lax.axis_size("space"), lax.axis_size("tm")
    far = [(i, (i + 1 if i % 2 else i - 1) % count) for i in range(count)]
    near = [(i, i ^ 1) for i in range(count)]
    mixed = [
        (t * count + a, t * count + b)
        for t in range(groups)
        for a, b in (far if t < among else near)
    ]
    from_far = lax.ppermute(block, ("tm", "space"), mixed)
    from_near = lax.ppermute(block, "space", near)
    return from_near, from_far


def forward(groups, distance):
    pairs = [(i, (i + distance) % groups) for i in range(groups)]
    if distance == 2 and groups > 2:
        pairs[-2:] = [(groups - 2, 1), (groups - 1, 0)]
    return pairs


def step(c_state):
    own = c_state[0]
    rows, cols = own.shape[1:]
    count, groups = lax.axis_size("space"), lax.axis_size("tm")
    assert rows == HALO == ROWS and count % 2 == 0
    full, half = jnp.float32, jnp.bfloat16
    inner, wide = rows // CF, cols // CF
    near, far = exchange(own, groups)
    own_here, own_sums, gather, spread = call(
        ready_kernel,
        [
            (own.shape, full),
            ((ROWS, cols), full),
            ((CF * LANES, LANES), half),
            ((LANES, CF * LANES), half),
        ],
        (own,),
        cost=4_000_000,
        hbm=(0,),
        scratch=[pltpu.SemaphoreType.DMA],
    )
    edges = ((FSTEPS, *own.shape), full)
    first, second, kept, means = call(
        near_kernel,
        [edges, edges, (own.shape, full), ((2 * ROWS, wide), full)],
        (near, own_here, own_sums, gather),
        cost=8_000_000,
    )
    end, sent, ends = call(
        far_kernel,
        [(own.shape, full), ((2, inner + 2 * EXT, wide), full), ((2, inner, wide), full)],
        (far, first, second, means, gather),
        cost=2_000_000,
    )
    reach = groups - 1
    depth = -(-(reach - EXT) // inner)
    pieces = [sent, *exchange(sent, groups - 1 - EXT)]
    for d in range(2, depth + 1):
        for sign in (1, -1):
            pairs = [(i, (i + sign * d) % count) for i in range(count)]
            pieces.append(lax.ppermute(sent, "space", pairs))
    (window,) = call(
        functools.partial(window_kernel, depth),
        [((2, inner * (2 * depth + 1) + 2 * EXT, wide), full)],
        pieces,
    )
    held = [sent]
    for k in range(1, groups):
        held.append(lax.ppermute(sent if k <= EXT else window, "tm", forward(groups, k)))
    whole = (own.shape, full)
    scratch = [pltpu.VMEM(own.shape, full), pltpu.SemaphoreType.DMA((OUT_PIECES,))]
    among = min(groups, 1 + EXT)
    (after,) = call(
        functools.partial(early_kernel, among),
        [whole],
        (kept, end, ends, spread, *held[:among]),
        cost=1_000_000,
        scratch=scratch,
        out=pl.BlockSpec(memory_space=pltpu.HBM),
    )
    if groups > among:
        (after,) = call(
            functools.partial(late_kernel, groups, among),
            [whole],
            (after, kept, end, ends, spread, *held),
            cost=1_000_000,
            hbm=(0,),
            scratch=scratch,
            out=pl.BlockSpec(memory_space=pltpu.HBM),
            alias={0: 0},
        )
    return after[None]


def solution(mesh):
    placed = (P("tm", None, "space", None),)
    return jax.shard_map(
        step, mesh=mesh, in_specs=placed, out_specs=P("tm", None, "space", None), check_vma=False
    )
```

```python
import functools

import jax
import jax.numpy as jnp
from jax import lax
from jax.experimental import pallas as pl
from jax.experimental.pallas import tpu as pltpu
from jax.sharding import PartitionSpec as P


FSTEPS = 4
CF = 4
COURANT = 0.06
DIFFUSION = 0.04
COARSE_COURANT = COURANT * FSTEPS / CF
COARSE_DIFFUSION = DIFFUSION * FSTEPS / (CF * CF)
EXT = 1
HALO = FSTEPS + CF * EXT
LANES = 128
VMEM = pl.BlockSpec(memory_space=pltpu.VMEM)
ROWS = 8
OUT_PIECES = 2


def shifted(field, amount, axis):
    return pltpu.roll(field, amount % field.shape[axis], axis)


def advance(fields, courant, diffusion, pitch):
    u, v = fields
    along_u, along_v = courant * u, courant * v
    above = jnp.maximum(along_u, 0.0) + diffusion
    below = above - along_u
    left = jnp.maximum(along_v, 0.0) + diffusion
    right = left - along_v
    center = 1.0 - ((above + below) + (left + right))
    return [
        center * q
        + (above * shifted(q, pitch, 0) + below * shifted(q, -pitch, 0))
        + (left * shifted(q, 1, 1) + right * shifted(q, -1, 1))
        for q in fields
    ]


def exact_dot(field, weights):
    total = None
    for part in range(3):
        piece = field.astype(jnp.bfloat16)
        if part < 2:
            field = field - piece.astype(jnp.float32)
        product = jnp.dot(piece, weights, preferred_element_type=jnp.float32)
        total = product if total is None else total + product
    return total


def block_weights(shape, value):
    long = 0 if shape[0] > shape[1] else 1
    at = lax.broadcasted_iota(jnp.int32, shape, long)
    to = lax.broadcasted_iota(jnp.int32, shape, 1 - long)
    return jnp.where(at // CF == to, value, 0.0).astype(jnp.bfloat16)


def by_pieces(field, weights):
    width, count = weights.shape[0], field.shape[0]
    pieces = [field[:, at : at + width] for at in range(0, field.shape[1], width)]
    done = exact_dot(jnp.concatenate(pieces, axis=0), weights)
    return jnp.concatenate([done[i * count : (i + 1) * count] for i in range(len(pieces))], axis=1)


def packed_sums(tiles):
    packed = None
    for i, tile in enumerate(tiles):
        total = tile + shifted(tile, -1, 0)
        total = total + shifted(total, -2, 0)
        if packed is None:
            packed = total
        else:
            row = lax.broadcasted_iota(jnp.int32, tile.shape, 0)
            packed = jnp.where(row % CF == i, shifted(total, i, 0), packed)
    return packed


def sums_of(means, i):
    return [means[i : i + 1], means[CF + i : CF + i + 1]]


def repeat_rows(first, second):
    cols = first.shape[1]
    row = lax.broadcasted_iota(jnp.int32, (ROWS, cols), 0)
    return jnp.where(
        row < CF, jnp.broadcast_to(first, (ROWS, cols)), jnp.broadcast_to(second, (ROWS, cols))
    )


def ready_kernel(own_hbm, own_ref, sums_ref, gather_ref, spread_ref, sem):
    load = pltpu.make_async_copy(own_hbm, own_ref, sem)
    load.start()
    gather_ref[...] = block_weights(gather_ref.shape, 1.0 / (CF * CF))
    spread_ref[...] = block_weights(spread_ref.shape, 1.0)
    load.wait()
    sums_ref[...] = packed_sums([own_ref[0], own_ref[1]])


def near_kernel(
    near_ref, own_ref, sums_ref, gather_ref, first_ref, second_ref, kept_ref, means_ref
):
    odd = lax.axis_index("space") % 2 == 1
    fields = []
    for q in range(2):
        near, own = near_ref[q], own_ref[q]
        low, high = jnp.where(odd, near, own), jnp.where(odd, own, near)
        fields.append(jnp.concatenate([low, high], axis=0))
    near_sums = packed_sums([near_ref[0], near_ref[1]])
    row = lax.broadcasted_iota(jnp.int32, near_sums.shape, 0)
    near_sums = jnp.where(row % CF < 2, near_sums, shifted(sums_ref[...], 2, 0))
    for k in range(1, FSTEPS + 1):
        for q in range(2):
            own = jnp.where(odd, fields[q][ROWS:], fields[q][:ROWS])
            first_ref[k - 1, q] = pltpu.roll(own, jnp.where(odd, k, ROWS - k), 0)
            second_ref[k - 1, q] = pltpu.roll(own, jnp.where(odd, k + 1, ROWS - 1 - k), 0)
        fields = advance(fields, COURANT, DIFFUSION, 1)
    kept = [shifted(q, -CF, 0)[:ROWS] for q in fields]
    for q in range(2):
        kept_ref[q] = kept[q]
    end_sums = packed_sums(kept)
    both = by_pieces(jnp.concatenate([near_sums, end_sums], axis=0), gather_ref[...])
    means_ref[...] = both


def slanted(outer, first, second, odd):
    sign = jnp.where(odd, 1.0, -1.0)
    turn = jnp.where(odd, 1, ROWS - 1)
    row = lax.broadcasted_iota(jnp.int32, outer[0].shape, 0)
    edge = row == jnp.where(odd, 0, ROWS - 1)
    fields = [jnp.where(edge, first[q], pltpu.roll(outer[q], turn, 0)) for q in range(2)]
    inner = [jnp.where(edge, second[q], pltpu.roll(fields[q], turn, 0)) for q in range(2)]
    along_u, along_v = (sign * COURANT) * fields[0], COURANT * fields[1]
    toward = jnp.maximum(along_u, 0.0) + DIFFUSION
    away = toward - along_u
    left = jnp.maximum(along_v, 0.0) + DIFFUSION
    right = left - along_v
    center = 1.0 - ((toward + away) + (left + right))
    return [
        center * fields[q]
        + (toward * inner[q] + away * outer[q])
        + (left * shifted(fields[q], 1, 1) + right * shifted(fields[q], -1, 1))
        for q in range(2)
    ]


def window_means(ends, starts, gather):
    packed = packed_sums(ends)
    row = lax.broadcasted_iota(jnp.int32, packed.shape, 0)
    packed = jnp.where(row % CF < 2, packed, shifted(packed_sums(starts), 2, 0))
    return by_pieces(packed, gather)


def passed_on(end, start, first_group):
    coarse = advance(start, COARSE_COURANT, COARSE_DIFFUSION, 1)
    defects = [end[q] - coarse[q] for q in range(2)]
    return [jnp.where(first_group, coarse[q] + defects[q], defects[q]) for q in range(2)]


def far_kernel(
    far_ref, first_ref, second_ref, means_ref, gather_ref, end_ref, sent_ref, ends_ref, trail_ref, far_means_ref
):
    odd = lax.axis_index("space") % 2 == 1
    first_group = lax.axis_index("tm") == 0
    fields = [far_ref[0], far_ref[1]]
    for k in range(FSTEPS):
        fields = slanted(fields, first_ref[k], second_ref[k], odd)
        if k < FSTEPS - 1:
            for q in range(2):
                trail_ref[k, q] = fields[q]
    for q in range(2):
        end_ref[q] = fields[q]
    far_means = window_means(fields, [far_ref[0], far_ref[1]], gather_ref[...])
    far_means_ref[...] = far_means
    means = means_ref[...]
    near_means, near_ends = means[:ROWS], means[ROWS:]
    start, end = [], []
    for q in range(2):
        near, own, far = sums_of(near_means, q), sums_of(near_means, 2 + q), sums_of(far_means, 2 + q)
        this, that = sums_of(near_ends, q), sums_of(far_means, q)
        none = jnp.zeros_like(own[0])
        low = [jnp.where(odd, near[i], far[i]) for i in range(2)]
        high = [jnp.where(odd, far[i], near[i]) for i in range(2)]
        start.append(jnp.concatenate([*low, *own, *high, none, none], axis=0))
        low = [jnp.where(odd, this[i], that[i]) for i in range(2)]
        high = [jnp.where(odd, that[i], this[i]) for i in range(2)]
        end.append(jnp.concatenate([none, *low, *high, none, none, none], axis=0))
        ends_ref[q] = jnp.concatenate([low[1], high[0]], axis=0)
    sent = passed_on(end, start, first_group)
    for q in range(2):
        sent_ref[q] = sent[q][EXT : EXT + 2 + 2 * EXT]


def outer_kernel(
    among, far_ref, trail_ref, farther_ref, far_means_ref, gather_ref, sent_ref, near_ref, window_ref
):
    odd = lax.axis_index("space") % 2 == 1
    turn = jnp.where(odd, 1, ROWS - 1)
    group = lax.axis_index("tm")

    @pl.when(group >= among)
    def _():
        window_ref[...] = jnp.zeros_like(window_ref)

    @pl.when(group < among)
    def _():
        fields = [farther_ref[0], farther_ref[1]]
        for k in range(FSTEPS):
            beside = far_ref if k == 0 else trail_ref.at[k - 1]
            first = [pltpu.roll(beside[q], turn, 0) for q in range(2)]
            second = [pltpu.roll(first[q], turn, 0) for q in range(2)]
            fields = slanted(fields, first, second, odd)
        outer_means = window_means(fields, [farther_ref[0], farther_ref[1]], gather_ref[...])
        far_means = far_means_ref[...]
        start, end = [], []
        for q in range(2):
            far, farther = sums_of(far_means, 2 + q), sums_of(outer_means, 2 + q)
            none = jnp.zeros_like(far[0])
            low = [jnp.where(odd, far[i], farther[i]) for i in range(2)]
            high = [jnp.where(odd, farther[i], far[i]) for i in range(2)]
            start.append(jnp.concatenate([*low, *high] + [none] * 4, axis=0))
            end.append(jnp.concatenate([none, *sums_of(outer_means, q)] + [none] * 5, axis=0))
        added = passed_on(end, start, group == 0)
        for q in range(2):
            rows = added[q][1:3]
            low = jnp.where(odd, near_ref[q, :2], rows)
            high = jnp.where(odd, rows, near_ref[q, 2:])
            window_ref[q] = jnp.concatenate([low, sent_ref[q], high], axis=0)


def window_kernel(depth, own_ref, near_ref, far_ref, *rest):
    others, window_ref = rest[:-1], rest[-1]
    odd = lax.axis_index("space") % 2 == 1
    inner = own_ref.shape[1] - 2 * EXT
    for q in range(2):
        near, far = near_ref[q], far_ref[q]
        low, high = [jnp.where(odd, near, far)], [jnp.where(odd, far, near)]
        low += [others[2 * d][q] for d in range(depth - 1)]
        high += [others[2 * d + 1][q] for d in range(depth - 1)]
        parts = [low[-1][: EXT + inner]]
        parts += [part[EXT : EXT + inner] for part in reversed(low[:-1])]
        parts += [own_ref[q, EXT : EXT + inner]]
        parts += [part[EXT : EXT + inner] for part in high[:-1]]
        parts += [high[-1][EXT:]]
        window_ref[q] = jnp.concatenate(parts, axis=0)


def corrected(group, groups, held, kept_ref, end_ref, ends_ref, spread_ref, out_hbm, stage_ref, sems):
    reach = max(ref.shape[1] for ref in held)

    def placed(ref, q):
        term = ref[q]
        spare = (reach - term.shape[0]) // 2
        if spare:
            none = jnp.zeros((spare, term.shape[1]), jnp.float32)
            term = jnp.concatenate([none, term, none], axis=0)
        return term

    terms = [[placed(ref, q) for q in range(2)] for ref in held]

    def of(index):
        if index == groups - 1:
            return terms[0]
        picked = terms[min(len(terms) - 1, groups - 1 - index)]
        for k in range(min(len(terms) - 1, groups - 1 - index) - 1, -1, -1):
            picked = [jnp.where(group == index + k, terms[k][q], picked[q]) for q in range(2)]
        return picked

    path = of(0)
    for index in range(1, groups):
        term = of(index)
        after = advance(path, COARSE_COURANT, COARSE_DIFFUSION, 1)
        path = [jnp.where(index <= group, after[q] + term[q], path[q]) for q in range(2)]
    first = (reach - 2) // 2
    odd = lax.axis_index("space") % 2 == 1
    moves, own = [], []
    for q in range(2):
        move = path[q][first : first + 2] - ends_ref[q]
        moves.append(repeat_rows(move[:1], move[1:]))
        upper = lax.broadcasted_iota(jnp.int32, kept_ref.shape[1:], 0) >= CF
        own.append(shifted(jnp.where(upper == odd, kept_ref[q], end_ref[q]), CF, 0))
    lifted = by_pieces(jnp.concatenate(moves, axis=0), spread_ref[...])
    copies = []
    width = out_hbm.shape[2] // OUT_PIECES
    for i in range(OUT_PIECES):
        cols = slice(i * width, (i + 1) * width)
        for q in range(2):
            stage_ref[q, :, cols] = own[q][:, cols] + lifted[q * ROWS : (q + 1) * ROWS, cols]
        copy = pltpu.make_async_copy(stage_ref.at[:, :, cols], out_hbm.at[:, :, cols], sems.at[i])
        copy.start()
        copies.append(copy)
    for copy in copies:
        copy.wait()


def early_kernel(among, kept_ref, end_ref, ends_ref, spread_ref, *rest):
    held, (out_hbm, stage_ref, sems) = rest[:-3], rest[-3:]
    group = lax.axis_index("tm")

    @pl.when(group < among)
    def _():
        corrected(
            group, among, held, kept_ref, end_ref, ends_ref, spread_ref, out_hbm, stage_ref, sems
        )


def late_kernel(groups, among, before_hbm, kept_ref, end_ref, ends_ref, spread_ref, *rest):
    held, (out_hbm, stage_ref, sems) = rest[:-3], rest[-3:]
    group = lax.axis_index("tm")

    @pl.when(group >= among)
    def _():
        corrected(
            group, groups, held, kept_ref, end_ref, ends_ref, spread_ref, out_hbm, stage_ref, sems
        )


def call(kernel, shapes, operands, cost=0, hbm=(), scratch=(), out=VMEM, alias=None):
    where = [pl.BlockSpec(memory_space=pl.ANY) if i in hbm else VMEM for i in range(len(operands))]
    return pl.pallas_call(
        kernel,
        out_shape=[jax.ShapeDtypeStruct(shape, dtype) for shape, dtype in shapes],
        in_specs=where,
        out_specs=[out] * len(shapes),
        input_output_aliases=alias or {},
        scratch_shapes=scratch,
        cost_estimate=pl.CostEstimate(flops=cost, bytes_accessed=cost // 8, transcendentals=0),
        compiler_params=pltpu.CompilerParams(vmem_limit_bytes=16 * 1024 * 1024),
    )(*operands)


def from_near(block):
    pairs = [(i, i ^ 1) for i in range(lax.axis_size("space"))]
    return lax.ppermute(block, "space", pairs)


def from_far(block, step, among):
    count, groups = lax.axis_size("space"), lax.axis_size("tm")
    pairs = []
    for t in range(groups):
        for i in range(count):
            away = step if (i + step) % 2 == 0 else -step
            to = (i + away) % count if t < among else i ^ 1
            pairs.append((t * count + i, t * count + to))
    return lax.ppermute(block, ("tm", "space"), pairs)


def forward(groups, distance):
    return [(i, (i + distance) % groups) for i in range(groups)]


def step(c_state):
    own = c_state[0]
    rows, cols = own.shape[1:]
    count, groups = lax.axis_size("space"), lax.axis_size("tm")
    assert rows == HALO == ROWS and count % 2 == 0
    full, half = jnp.float32, jnp.bfloat16
    inner, wide = rows // CF, cols // CF
    reach, among = groups - 1, groups - 1 - EXT
    depth = -(-(reach - EXT) // inner)
    far = from_far(own, 1, groups)
    near = from_near(own)
    farther = from_far(own, 2, among) if depth == 1 else None
    own_here, own_sums, gather, spread = call(
        ready_kernel,
        [
            (own.shape, full),
            ((ROWS, cols), full),
            ((CF * LANES, LANES), half),
            ((LANES, CF * LANES), half),
        ],
        (own,),
        cost=4_000_000,
        hbm=(0,),
        scratch=[pltpu.SemaphoreType.DMA],
    )
    edges = ((FSTEPS, *own.shape), full)
    first, second, kept, means = call(
        near_kernel,
        [edges, edges, (own.shape, full), ((2 * ROWS, wide), full)],
        (near, own_here, own_sums, gather),
        cost=8_000_000,
    )
    sent_shape = (2, inner + 2 * EXT, wide)
    end, sent, ends, trail, far_means = call(
        far_kernel,
        [
            (own.shape, full),
            (sent_shape, full),
            ((2, inner, wide), full),
            ((FSTEPS - 1, *own.shape), full),
            ((ROWS, wide), full),
        ],
        (far, first, second, means, gather),
        cost=2_000_000,
    )
    near_rows = from_near(sent)
    window = ((2, inner * (2 * depth + 1) + 2 * EXT, wide), full)
    if depth == 1:
        (window,) = call(
            functools.partial(outer_kernel, among),
            [window],
            (far, trail, farther, far_means, gather, sent, near_rows),
            cost=2_000_000,
        )
    else:
        pieces = [sent, near_rows, from_far(sent, 1, among)]
        for d in range(2, depth + 1):
            for sign in (1, -1):
                pairs = [(i, (i + sign * d) % count) for i in range(count)]
                pieces.append(lax.ppermute(sent, "space", pairs))
        (window,) = call(functools.partial(window_kernel, depth), [window], pieces)
    held = [sent]
    for k in range(1, groups):
        held.append(lax.ppermute(sent if k <= EXT else window, "tm", forward(groups, k)))
    whole = (own.shape, full)
    scratch = [pltpu.VMEM(own.shape, full), pltpu.SemaphoreType.DMA((OUT_PIECES,))]
    early = min(groups, 1 + EXT)
    (after,) = call(
        functools.partial(early_kernel, early),
        [whole],
        (kept, end, ends, spread, *held[:early]),
        cost=1_000_000,
        scratch=scratch,
        out=pl.BlockSpec(memory_space=pltpu.HBM),
    )
    if groups > early:
        (after,) = call(
            functools.partial(late_kernel, groups, early),
            [whole],
            (after, kept, end, ends, spread, *held),
            cost=1_000_000,
            hbm=(0,),
            scratch=scratch,
            out=pl.BlockSpec(memory_space=pltpu.HBM),
            alias={0: 0},
        )
    return after[None]


def solution(mesh):
    placed = (P("tm", None, "space", None),)
    return jax.shard_map(
        step, mesh=mesh, in_specs=placed, out_specs=P("tm", None, "space", None), check_vma=False
    )
```

```python
import functools

import jax
import jax.numpy as jnp
from jax import lax
from jax.experimental import pallas as pl
from jax.experimental.pallas import tpu as pltpu
from jax.sharding import PartitionSpec as P


FSTEPS = 4
CF = 4
COURANT = 0.06
DIFFUSION = 0.04
COARSE_COURANT = COURANT * FSTEPS / CF
COARSE_DIFFUSION = DIFFUSION * FSTEPS / (CF * CF)
EXT = 1
HALO = FSTEPS + CF * EXT
LANES = 128
VMEM = pl.BlockSpec(memory_space=pltpu.VMEM)
ROWS = 8
OUT_PIECES = 2


def shifted(field, amount, axis):
    return pltpu.roll(field, amount % field.shape[axis], axis)


def advance(fields, courant, diffusion, pitch):
    u, v = fields
    along_u, along_v = courant * u, courant * v
    above = jnp.maximum(along_u, 0.0) + diffusion
    below = above - along_u
    left = jnp.maximum(along_v, 0.0) + diffusion
    right = left - along_v
    center = 1.0 - ((above + below) + (left + right))
    return [
        center * q
        + (above * shifted(q, pitch, 0) + below * shifted(q, -pitch, 0))
        + (left * shifted(q, 1, 1) + right * shifted(q, -1, 1))
        for q in fields
    ]


def exact_dot(field, weights):
    parts = []
    for part in range(3):
        piece = field.astype(jnp.bfloat16)
        parts.append(piece)
        if part < 2:
            field = field - piece.astype(jnp.float32)
    count = field.shape[0]
    done = jnp.dot(jnp.concatenate(parts, axis=0), weights, preferred_element_type=jnp.float32)
    return done[:count] + (done[count : 2 * count] + done[2 * count :])


def block_weights(shape, value):
    long = 0 if shape[0] > shape[1] else 1
    at = lax.broadcasted_iota(jnp.int32, shape, long)
    to = lax.broadcasted_iota(jnp.int32, shape, 1 - long)
    return jnp.where(at // CF == to, value, 0.0).astype(jnp.bfloat16)


def by_pieces(field, weights):
    width, count = weights.shape[0], field.shape[0]
    pieces = [field[:, at : at + width] for at in range(0, field.shape[1], width)]
    done = exact_dot(jnp.concatenate(pieces, axis=0), weights)
    return jnp.concatenate([done[i * count : (i + 1) * count] for i in range(len(pieces))], axis=1)


def packed_sums(tiles):
    packed = None
    for i, tile in enumerate(tiles):
        total = tile + shifted(tile, -1, 0)
        total = total + shifted(total, -2, 0)
        if packed is None:
            packed = total
        else:
            row = lax.broadcasted_iota(jnp.int32, tile.shape, 0)
            packed = jnp.where(row % CF == i, shifted(total, i, 0), packed)
    return packed


def place(base, tile, odd, moves):
    row = lax.broadcasted_iota(jnp.int32, base.shape, 0)
    for source, on_odd, on_even in moves:
        turned = pltpu.roll(tile, jnp.where(odd, (on_odd - source) % ROWS, (on_even - source) % ROWS), 0)
        base = jnp.where(row == jnp.where(odd, on_odd, on_even), turned, base)
    return base


def repeat_rows(first, second):
    cols = first.shape[1]
    row = lax.broadcasted_iota(jnp.int32, (ROWS, cols), 0)
    return jnp.where(
        row < CF, jnp.broadcast_to(first, (ROWS, cols)), jnp.broadcast_to(second, (ROWS, cols))
    )


def ready_kernel(own_hbm, own_ref, sums_ref, gather_ref, spread_ref, sem):
    load = pltpu.make_async_copy(own_hbm, own_ref, sem)
    load.start()
    gather_ref[...] = block_weights(gather_ref.shape, 1.0 / (CF * CF))
    spread_ref[...] = block_weights(spread_ref.shape, 1.0)
    load.wait()
    sums_ref[...] = packed_sums([own_ref[0], own_ref[1]])


def near_kernel(
    near_ref, own_ref, sums_ref, gather_ref, first_ref, second_ref, kept_ref, start_ref, end_ref
):
    odd = lax.axis_index("space") % 2 == 1
    fields = []
    for q in range(2):
        near, own = near_ref[q], own_ref[q]
        low, high = jnp.where(odd, near, own), jnp.where(odd, own, near)
        fields.append(jnp.concatenate([low, high], axis=0))
    near_sums = packed_sums([near_ref[0], near_ref[1]])
    row = lax.broadcasted_iota(jnp.int32, near_sums.shape, 0)
    near_sums = jnp.where(row % CF < 2, near_sums, shifted(sums_ref[...], 2, 0))
    for k in range(1, FSTEPS + 1):
        for q in range(2):
            own = jnp.where(odd, fields[q][ROWS:], fields[q][:ROWS])
            first_ref[k - 1, q] = pltpu.roll(own, jnp.where(odd, k, ROWS - k), 0)
            second_ref[k - 1, q] = pltpu.roll(own, jnp.where(odd, k + 1, ROWS - 1 - k), 0)
        fields = advance(fields, COURANT, DIFFUSION, 1)
    kept = [shifted(q, -CF, 0)[:ROWS] for q in fields]
    for q in range(2):
        kept_ref[q] = kept[q]
    end_sums = packed_sums(kept)
    both = by_pieces(jnp.concatenate([near_sums, end_sums], axis=0), gather_ref[...])
    begun, ended = both[:ROWS], both[ROWS:]
    none = jnp.zeros_like(begun)
    for q in range(2):
        own = ((2 + q, 1, 1), (CF + 2 + q, 2, 2))
        start_ref[q] = place(none, begun, odd, ((q, 7, 3), (CF + q, 0, 4), *own))
        end_ref[q] = place(none, ended, odd, ((q, 0, 2), (CF + q, 1, 3)))


def slanted(outer, first, second, odd):
    sign = jnp.where(odd, 1.0, -1.0)
    turn = jnp.where(odd, 1, ROWS - 1)
    row = lax.broadcasted_iota(jnp.int32, outer[0].shape, 0)
    edge = row == jnp.where(odd, 0, ROWS - 1)
    fields = [jnp.where(edge, first[q], pltpu.roll(outer[q], turn, 0)) for q in range(2)]
    inner = [jnp.where(edge, second[q], pltpu.roll(fields[q], turn, 0)) for q in range(2)]
    along_u, along_v = (sign * COURANT) * fields[0], COURANT * fields[1]
    toward = jnp.maximum(along_u, 0.0) + DIFFUSION
    away = toward - along_u
    left = jnp.maximum(along_v, 0.0) + DIFFUSION
    right = left - along_v
    center = 1.0 - ((toward + away) + (left + right))
    return [
        center * fields[q]
        + (toward * inner[q] + away * outer[q])
        + (left * shifted(fields[q], 1, 1) + right * shifted(fields[q], -1, 1))
        for q in range(2)
    ]


def window_means(ends, starts, gather):
    packed = packed_sums(ends)
    row = lax.broadcasted_iota(jnp.int32, packed.shape, 0)
    packed = jnp.where(row % CF < 2, packed, shifted(packed_sums(starts), 2, 0))
    return by_pieces(packed, gather)


def passed_on(end, start, first_group):
    coarse = advance(start, COARSE_COURANT, COARSE_DIFFUSION, 1)
    defects = [end[q] - coarse[q] for q in range(2)]
    return [jnp.where(first_group, coarse[q] + defects[q], defects[q]) for q in range(2)]


def far_kernel(
    far_ref,
    first_ref,
    second_ref,
    near_start_ref,
    near_end_ref,
    gather_ref,
    end_ref,
    sent_ref,
    ends_ref,
    trail_ref,
    far_means_ref,
):
    odd = lax.axis_index("space") % 2 == 1
    first_group = lax.axis_index("tm") == 0
    fields = [far_ref[0], far_ref[1]]
    for k in range(FSTEPS):
        fields = slanted(fields, first_ref[k], second_ref[k], odd)
        if k < FSTEPS - 1:
            for q in range(2):
                trail_ref[k, q] = fields[q]
    for q in range(2):
        end_ref[q] = fields[q]
    far_means = window_means(fields, [far_ref[0], far_ref[1]], gather_ref[...])
    far_means_ref[...] = far_means
    start, end = [], []
    for q in range(2):
        moves = ((2 + q, 3, 7), (CF + 2 + q, 4, 0))
        start.append(place(near_start_ref[q], far_means, odd, moves))
        end.append(place(near_end_ref[q], far_means, odd, ((q, 2, 0), (CF + q, 3, 1))))
    sent = passed_on(end, start, first_group)
    for q in range(2):
        sent_ref[q] = sent[q][: 2 + 2 * EXT]
        ends_ref[q] = end[q]


def outer_kernel(
    among, far_ref, trail_ref, farther_ref, far_means_ref, gather_ref, sent_ref, near_ref, window_ref
):
    odd = lax.axis_index("space") % 2 == 1
    turn = jnp.where(odd, 1, ROWS - 1)
    group = lax.axis_index("tm")

    @pl.when(group >= among)
    def _():
        window_ref[...] = jnp.zeros_like(window_ref)

    @pl.when(group < among)
    def _():
        fields = [farther_ref[0], farther_ref[1]]
        for k in range(FSTEPS):
            beside = far_ref if k == 0 else trail_ref.at[k - 1]
            first = [pltpu.roll(beside[q], turn, 0) for q in range(2)]
            second = [pltpu.roll(first[q], turn, 0) for q in range(2)]
            fields = slanted(fields, first, second, odd)
        outer_means = window_means(fields, [farther_ref[0], farther_ref[1]], gather_ref[...])
        none = jnp.zeros((ROWS, outer_means.shape[1]), jnp.float32)
        gap = none[:2]
        start, end, window = [], [], []
        for q in range(2):
            begun = place(none, far_means_ref[...], odd, ((2 + q, 5, 1), (CF + 2 + q, 6, 2)))
            moves = ((2 + q, 7, 7), (CF + 2 + q, 0, 0))
            start.append(place(begun, outer_means, odd, moves))
            end.append(place(none, outer_means, odd, ((q, 6, 0), (CF + q, 7, 1))))
            beside = jnp.concatenate([near_ref[q], near_ref[q]], axis=0)
            middle = jnp.concatenate([gap, sent_ref[q], gap], axis=0)
            row = lax.broadcasted_iota(jnp.int32, none.shape, 0)
            window.append(jnp.where((row >= 2) & (row < 6), middle, beside))
        added = passed_on(end, start, group == 0)
        fresh = (row >= 6) == odd
        inside = (row >= 2) & (row < 6)
        for q in range(2):
            window_ref[q] = jnp.where(fresh & jnp.logical_not(inside), added[q], window[q])


def window_kernel(depth, own_ref, near_ref, far_ref, *rest):
    others, window_ref = rest[:-1], rest[-1]
    odd = lax.axis_index("space") % 2 == 1
    inner = own_ref.shape[1] - 2 * EXT
    for q in range(2):
        near, far = near_ref[q], far_ref[q]
        low, high = [jnp.where(odd, near, far)], [jnp.where(odd, far, near)]
        low += [others[2 * d][q] for d in range(depth - 1)]
        high += [others[2 * d + 1][q] for d in range(depth - 1)]
        parts = [low[-1][: EXT + inner]]
        parts += [part[EXT : EXT + inner] for part in reversed(low[:-1])]
        parts += [own_ref[q, EXT : EXT + inner]]
        parts += [part[EXT : EXT + inner] for part in high[:-1]]
        parts += [high[-1][EXT:]]
        window_ref[q] = jnp.concatenate(parts, axis=0)


def corrected(group, groups, held, kept_ref, end_ref, ends_ref, spread_ref, out_hbm, stage_ref, sems):
    reach = max(ref.shape[1] for ref in held)

    def placed(ref, q):
        term = ref[q]
        spare = (reach - term.shape[0]) // 2
        if spare:
            none = jnp.zeros((spare, term.shape[1]), jnp.float32)
            term = jnp.concatenate([none, term, none], axis=0)
        return term

    terms = [[placed(ref, q) for q in range(2)] for ref in held]

    def of(index):
        if index == groups - 1:
            return terms[0]
        picked = terms[min(len(terms) - 1, groups - 1 - index)]
        for k in range(min(len(terms) - 1, groups - 1 - index) - 1, -1, -1):
            picked = [jnp.where(group == index + k, terms[k][q], picked[q]) for q in range(2)]
        return picked

    path = of(0)
    for index in range(1, groups):
        term = of(index)
        after = advance(path, COARSE_COURANT, COARSE_DIFFUSION, 1)
        path = [jnp.where(index <= group, after[q] + term[q], path[q]) for q in range(2)]
    first = (reach - 2) // 2
    odd = lax.axis_index("space") % 2 == 1
    moves, own = [], []
    for q in range(2):
        move = path[q][first : first + 2] - ends_ref[q, EXT : EXT + 2]
        moves.append(repeat_rows(move[:1], move[1:]))
        upper = lax.broadcasted_iota(jnp.int32, kept_ref.shape[1:], 0) >= CF
        own.append(shifted(jnp.where(upper == odd, kept_ref[q], end_ref[q]), CF, 0))
    lifted = by_pieces(jnp.concatenate(moves, axis=0), spread_ref[...])
    copies = []
    width = out_hbm.shape[2] // OUT_PIECES
    for i in range(OUT_PIECES):
        cols = slice(i * width, (i + 1) * width)
        for q in range(2):
            stage_ref[q, :, cols] = own[q][:, cols] + lifted[q * ROWS : (q + 1) * ROWS, cols]
        copy = pltpu.make_async_copy(stage_ref.at[:, :, cols], out_hbm.at[:, :, cols], sems.at[i])
        copy.start()
        copies.append(copy)
    for copy in copies:
        copy.wait()


def early_kernel(among, kept_ref, end_ref, ends_ref, spread_ref, *rest):
    held, (out_hbm, stage_ref, sems) = rest[:-3], rest[-3:]
    group = lax.axis_index("tm")

    @pl.when(group < among)
    def _():
        corrected(
            group, among, held, kept_ref, end_ref, ends_ref, spread_ref, out_hbm, stage_ref, sems
        )


def late_kernel(groups, among, before_hbm, kept_ref, end_ref, ends_ref, spread_ref, *rest):
    held, (out_hbm, stage_ref, sems) = rest[:-3], rest[-3:]
    group = lax.axis_index("tm")

    @pl.when(group >= among)
    def _():
        corrected(
            group, groups, held, kept_ref, end_ref, ends_ref, spread_ref, out_hbm, stage_ref, sems
        )


def call(kernel, shapes, operands, cost=0, hbm=(), scratch=(), out=VMEM, alias=None):
    where = [pl.BlockSpec(memory_space=pl.ANY) if i in hbm else VMEM for i in range(len(operands))]
    return pl.pallas_call(
        kernel,
        out_shape=[jax.ShapeDtypeStruct(shape, dtype) for shape, dtype in shapes],
        in_specs=where,
        out_specs=[out] * len(shapes),
        input_output_aliases=alias or {},
        scratch_shapes=scratch,
        cost_estimate=pl.CostEstimate(flops=cost, bytes_accessed=cost // 8, transcendentals=0),
        compiler_params=pltpu.CompilerParams(vmem_limit_bytes=16 * 1024 * 1024),
    )(*operands)


def from_near(block):
    pairs = [(i, i ^ 1) for i in range(lax.axis_size("space"))]
    return lax.ppermute(block, "space", pairs)


def from_far(block, step, among):
    count, groups = lax.axis_size("space"), lax.axis_size("tm")
    pairs = []
    for t in range(groups):
        for i in range(count):
            away = step if (i + step) % 2 == 0 else -step
            to = (i + away) % count if t < among else i ^ 1
            pairs.append((t * count + i, t * count + to))
    return lax.ppermute(block, ("tm", "space"), pairs)


def forward(groups, distance):
    return [(i, (i + distance) % groups) for i in range(groups)]


def step(c_state):
    own = c_state[0]
    rows, cols = own.shape[1:]
    count, groups = lax.axis_size("space"), lax.axis_size("tm")
    assert rows == HALO == ROWS and count % 2 == 0
    full, half = jnp.float32, jnp.bfloat16
    inner, wide = rows // CF, cols // CF
    reach, among = groups - 1, groups - 1 - EXT
    depth = -(-(reach - EXT) // inner)
    far = from_far(own, 1, groups)
    near = from_near(own)
    farther = from_far(own, 2, among) if depth == 1 else None
    own_here, own_sums, gather, spread = call(
        ready_kernel,
        [
            (own.shape, full),
            ((ROWS, cols), full),
            ((CF * LANES, LANES), half),
            ((LANES, CF * LANES), half),
        ],
        (own,),
        cost=4_000_000,
        hbm=(0,),
        scratch=[pltpu.SemaphoreType.DMA],
    )
    edges = ((FSTEPS, *own.shape), full)
    tile = ((2, ROWS, wide), full)
    first, second, kept, near_start, near_end = call(
        near_kernel,
        [edges, edges, (own.shape, full), tile, tile],
        (near, own_here, own_sums, gather),
        cost=8_000_000,
    )
    sent_shape = (2, inner + 2 * EXT, wide)
    end, sent, ends, trail, far_means = call(
        far_kernel,
        [
            (own.shape, full),
            (sent_shape, full),
            tile,
            ((FSTEPS - 1, *own.shape), full),
            ((ROWS, wide), full),
        ],
        (far, first, second, near_start, near_end, gather),
        cost=2_000_000,
    )
    near_rows = from_near(sent)
    window = ((2, inner * (2 * depth + 1) + 2 * EXT, wide), full)
    if depth == 1:
        (window,) = call(
            functools.partial(outer_kernel, among),
            [window],
            (far, trail, farther, far_means, gather, sent, near_rows),
            cost=2_000_000,
        )
    else:
        pieces = [sent, near_rows, from_far(sent, 1, among)]
        for d in range(2, depth + 1):
            for sign in (1, -1):
                pairs = [(i, (i + sign * d) % count) for i in range(count)]
                pieces.append(lax.ppermute(sent, "space", pairs))
        (window,) = call(functools.partial(window_kernel, depth), [window], pieces)
    held = [sent]
    for k in range(1, groups):
        held.append(lax.ppermute(sent if k <= EXT else window, "tm", forward(groups, k)))
    whole = (own.shape, full)
    scratch = [pltpu.VMEM(own.shape, full), pltpu.SemaphoreType.DMA((OUT_PIECES,))]
    early = min(groups, 1 + EXT)
    (after,) = call(
        functools.partial(early_kernel, early),
        [whole],
        (kept, end, ends, spread, *held[:early]),
        cost=1_000_000,
        scratch=scratch,
        out=pl.BlockSpec(memory_space=pltpu.HBM),
    )
    if groups > early:
        (after,) = call(
            functools.partial(late_kernel, groups, early),
            [whole],
            (after, kept, end, ends, spread, *held),
            cost=1_000_000,
            hbm=(0,),
            scratch=scratch,
            out=pl.BlockSpec(memory_space=pltpu.HBM),
            alias={0: 0},
        )
    return after[None]


def solution(mesh):
    placed = (P("tm", None, "space", None),)
    return jax.shard_map(
        step, mesh=mesh, in_specs=placed, out_specs=P("tm", None, "space", None), check_vma=False
    )
```

```python
import functools

import jax
import jax.numpy as jnp
from jax import lax
from jax.experimental import pallas as pl
from jax.experimental.pallas import tpu as pltpu
from jax.sharding import PartitionSpec as P


FSTEPS = 4
CF = 4
COURANT = 0.06
DIFFUSION = 0.04
COARSE_COURANT = COURANT * FSTEPS / CF
COARSE_DIFFUSION = DIFFUSION * FSTEPS / (CF * CF)
EXT = 1
HALO = FSTEPS + CF * EXT
LANES = 128
VMEM = pl.BlockSpec(memory_space=pltpu.VMEM)
ROWS = 8
OUT_PIECES = 2
HOLD_TURNS = 80


def shifted(field, amount, axis):
    return pltpu.roll(field, amount % field.shape[axis], axis)


def advance(fields, courant, diffusion, pitch):
    u, v = fields
    along_u, along_v = courant * u, courant * v
    above = jnp.maximum(along_u, 0.0) + diffusion
    below = above - along_u
    left = jnp.maximum(along_v, 0.0) + diffusion
    right = left - along_v
    center = 1.0 - ((above + below) + (left + right))
    return [
        center * q
        + (above * shifted(q, pitch, 0) + below * shifted(q, -pitch, 0))
        + (left * shifted(q, 1, 1) + right * shifted(q, -1, 1))
        for q in fields
    ]


def exact_dot(field, weights):
    parts = []
    for part in range(3):
        piece = field.astype(jnp.bfloat16)
        parts.append(piece)
        if part < 2:
            field = field - piece.astype(jnp.float32)
    count = field.shape[0]
    done = jnp.dot(jnp.concatenate(parts, axis=0), weights, preferred_element_type=jnp.float32)
    return done[:count] + (done[count : 2 * count] + done[2 * count :])


def block_weights(shape, value):
    long = 0 if shape[0] > shape[1] else 1
    at = lax.broadcasted_iota(jnp.int32, shape, long)
    to = lax.broadcasted_iota(jnp.int32, shape, 1 - long)
    return jnp.where(at // CF == to, value, 0.0).astype(jnp.bfloat16)


def by_pieces(field, weights):
    width, count = weights.shape[0], field.shape[0]
    pieces = [field[:, at : at + width] for at in range(0, field.shape[1], width)]
    done = exact_dot(jnp.concatenate(pieces, axis=0), weights)
    return jnp.concatenate([done[i * count : (i + 1) * count] for i in range(len(pieces))], axis=1)


def packed_sums(tiles):
    packed = None
    for i, tile in enumerate(tiles):
        total = tile + shifted(tile, -1, 0)
        total = total + shifted(total, -2, 0)
        if packed is None:
            packed = total
        else:
            row = lax.broadcasted_iota(jnp.int32, tile.shape, 0)
            packed = jnp.where(row % CF == i, shifted(total, i, 0), packed)
    return packed


def place(base, tile, odd, moves):
    row = lax.broadcasted_iota(jnp.int32, base.shape, 0)
    for source, on_odd, on_even in moves:
        turned = pltpu.roll(tile, jnp.where(odd, (on_odd - source) % ROWS, (on_even - source) % ROWS), 0)
        base = jnp.where(row == jnp.where(odd, on_odd, on_even), turned, base)
    return base


def repeat_rows(first, second):
    cols = first.shape[1]
    row = lax.broadcasted_iota(jnp.int32, (ROWS, cols), 0)
    return jnp.where(
        row < CF, jnp.broadcast_to(first, (ROWS, cols)), jnp.broadcast_to(second, (ROWS, cols))
    )


def ready_kernel(held_ref, own_hbm, own_ref, sums_ref, gather_ref, spread_ref, sem):
    load = pltpu.make_async_copy(own_hbm, own_ref, sem)
    load.start()
    gather_ref[...] = block_weights(gather_ref.shape, 1.0 / (CF * CF))
    spread_ref[...] = block_weights(spread_ref.shape, 1.0)
    load.wait()
    sums_ref[...] = packed_sums([own_ref[0], own_ref[1]])


def near_kernel(
    near_ref, own_ref, sums_ref, gather_ref, first_ref, second_ref, kept_ref, start_ref, end_ref
):
    odd = lax.axis_index("space") % 2 == 1
    fields = []
    for q in range(2):
        near, own = near_ref[q], own_ref[q]
        low, high = jnp.where(odd, near, own), jnp.where(odd, own, near)
        fields.append(jnp.concatenate([low, high], axis=0))
    near_sums = packed_sums([near_ref[0], near_ref[1]])
    row = lax.broadcasted_iota(jnp.int32, near_sums.shape, 0)
    near_sums = jnp.where(row % CF < 2, near_sums, shifted(sums_ref[...], 2, 0))
    for k in range(1, FSTEPS + 1):
        for q in range(2):
            own = jnp.where(odd, fields[q][ROWS:], fields[q][:ROWS])
            first_ref[k - 1, q] = pltpu.roll(own, jnp.where(odd, k, ROWS - k), 0)
            second_ref[k - 1, q] = pltpu.roll(own, jnp.where(odd, k + 1, ROWS - 1 - k), 0)
        fields = advance(fields, COURANT, DIFFUSION, 1)
    kept = [shifted(q, -CF, 0)[:ROWS] for q in fields]
    for q in range(2):
        kept_ref[q] = kept[q]
    end_sums = packed_sums(kept)
    both = by_pieces(jnp.concatenate([near_sums, end_sums], axis=0), gather_ref[...])
    begun, ended = both[:ROWS], both[ROWS:]
    none = jnp.zeros_like(begun)
    for q in range(2):
        own = ((2 + q, 1, 1), (CF + 2 + q, 2, 2))
        start_ref[q] = place(none, begun, odd, ((q, 7, 3), (CF + q, 0, 4), *own))
        end_ref[q] = place(none, ended, odd, ((q, 0, 2), (CF + q, 1, 3)))


def slanted(outer, first, second, odd):
    sign = jnp.where(odd, 1.0, -1.0)
    turn = jnp.where(odd, 1, ROWS - 1)
    row = lax.broadcasted_iota(jnp.int32, outer[0].shape, 0)
    edge = row == jnp.where(odd, 0, ROWS - 1)
    fields = [jnp.where(edge, first[q], pltpu.roll(outer[q], turn, 0)) for q in range(2)]
    inner = [jnp.where(edge, second[q], pltpu.roll(fields[q], turn, 0)) for q in range(2)]
    along_u, along_v = (sign * COURANT) * fields[0], COURANT * fields[1]
    toward = jnp.maximum(along_u, 0.0) + DIFFUSION
    away = toward - along_u
    left = jnp.maximum(along_v, 0.0) + DIFFUSION
    right = left - along_v
    center = 1.0 - ((toward + away) + (left + right))
    return [
        center * fields[q]
        + (toward * inner[q] + away * outer[q])
        + (left * shifted(fields[q], 1, 1) + right * shifted(fields[q], -1, 1))
        for q in range(2)
    ]


def window_means(ends, starts, gather):
    packed = packed_sums(ends)
    row = lax.broadcasted_iota(jnp.int32, packed.shape, 0)
    packed = jnp.where(row % CF < 2, packed, shifted(packed_sums(starts), 2, 0))
    return by_pieces(packed, gather)


def passed_on(end, start, first_group):
    coarse = advance(start, COARSE_COURANT, COARSE_DIFFUSION, 1)
    defects = [end[q] - coarse[q] for q in range(2)]
    return [jnp.where(first_group, coarse[q] + defects[q], defects[q]) for q in range(2)]


def far_kernel(
    far_ref,
    first_ref,
    second_ref,
    near_start_ref,
    near_end_ref,
    gather_ref,
    end_ref,
    sent_ref,
    ends_ref,
    trail_ref,
    far_means_ref,
):
    odd = lax.axis_index("space") % 2 == 1
    first_group = lax.axis_index("tm") == 0
    fields = [far_ref[0], far_ref[1]]
    for k in range(FSTEPS):
        fields = slanted(fields, first_ref[k], second_ref[k], odd)
        if k < FSTEPS - 1:
            for q in range(2):
                trail_ref[k, q] = fields[q]
    for q in range(2):
        end_ref[q] = fields[q]
    far_means = window_means(fields, [far_ref[0], far_ref[1]], gather_ref[...])
    far_means_ref[...] = far_means
    start, end = [], []
    for q in range(2):
        moves = ((2 + q, 3, 7), (CF + 2 + q, 4, 0))
        start.append(place(near_start_ref[q], far_means, odd, moves))
        end.append(place(near_end_ref[q], far_means, odd, ((q, 2, 0), (CF + q, 3, 1))))
    sent = passed_on(end, start, first_group)
    for q in range(2):
        sent_ref[q] = sent[q][: 2 + 2 * EXT]
        ends_ref[q] = end[q]


def outer_kernel(
    among, far_ref, trail_ref, farther_ref, far_means_ref, gather_ref, sent_ref, near_ref, window_ref
):
    odd = lax.axis_index("space") % 2 == 1
    turn = jnp.where(odd, 1, ROWS - 1)
    group = lax.axis_index("tm")

    @pl.when(group >= among)
    def _():
        window_ref[...] = jnp.zeros_like(window_ref)

    @pl.when(group < among)
    def _():
        fields = [farther_ref[0], farther_ref[1]]
        for k in range(FSTEPS):
            beside = far_ref if k == 0 else trail_ref.at[k - 1]
            first = [pltpu.roll(beside[q], turn, 0) for q in range(2)]
            second = [pltpu.roll(first[q], turn, 0) for q in range(2)]
            fields = slanted(fields, first, second, odd)
        outer_means = window_means(fields, [farther_ref[0], farther_ref[1]], gather_ref[...])
        none = jnp.zeros((ROWS, outer_means.shape[1]), jnp.float32)
        gap = none[:2]
        start, end, window = [], [], []
        for q in range(2):
            begun = place(none, far_means_ref[...], odd, ((2 + q, 5, 1), (CF + 2 + q, 6, 2)))
            moves = ((2 + q, 7, 7), (CF + 2 + q, 0, 0))
            start.append(place(begun, outer_means, odd, moves))
            end.append(place(none, outer_means, odd, ((q, 6, 0), (CF + q, 7, 1))))
            beside = jnp.concatenate([near_ref[q], near_ref[q]], axis=0)
            middle = jnp.concatenate([gap, sent_ref[q], gap], axis=0)
            row = lax.broadcasted_iota(jnp.int32, none.shape, 0)
            window.append(jnp.where((row >= 2) & (row < 6), middle, beside))
        added = passed_on(end, start, group == 0)
        fresh = (row >= 6) == odd
        inside = (row >= 2) & (row < 6)
        for q in range(2):
            window_ref[q] = jnp.where(fresh & jnp.logical_not(inside), added[q], window[q])


def window_kernel(depth, own_ref, near_ref, far_ref, *rest):
    others, window_ref = rest[:-1], rest[-1]
    odd = lax.axis_index("space") % 2 == 1
    inner = own_ref.shape[1] - 2 * EXT
    for q in range(2):
        near, far = near_ref[q], far_ref[q]
        low, high = [jnp.where(odd, near, far)], [jnp.where(odd, far, near)]
        low += [others[2 * d][q] for d in range(depth - 1)]
        high += [others[2 * d + 1][q] for d in range(depth - 1)]
        parts = [low[-1][: EXT + inner]]
        parts += [part[EXT : EXT + inner] for part in reversed(low[:-1])]
        parts += [own_ref[q, EXT : EXT + inner]]
        parts += [part[EXT : EXT + inner] for part in high[:-1]]
        parts += [high[-1][EXT:]]
        window_ref[q] = jnp.concatenate(parts, axis=0)


def corrected(group, groups, held, kept_ref, end_ref, ends_ref, spread_ref, out_hbm, stage_ref, sems):
    reach = max(ref.shape[1] for ref in held)

    def placed(ref, q):
        term = ref[q]
        spare = (reach - term.shape[0]) // 2
        if spare:
            none = jnp.zeros((spare, term.shape[1]), jnp.float32)
            term = jnp.concatenate([none, term, none], axis=0)
        return term

    terms = [[placed(ref, q) for q in range(2)] for ref in held]

    def of(index):
        if index == groups - 1:
            return terms[0]
        picked = terms[min(len(terms) - 1, groups - 1 - index)]
        for k in range(min(len(terms) - 1, groups - 1 - index) - 1, -1, -1):
            picked = [jnp.where(group == index + k, terms[k][q], picked[q]) for q in range(2)]
        return picked

    path = of(0)
    for index in range(1, groups):
        term = of(index)
        after = advance(path, COARSE_COURANT, COARSE_DIFFUSION, 1)
        path = [jnp.where(index <= group, after[q] + term[q], path[q]) for q in range(2)]
    first = (reach - 2) // 2
    odd = lax.axis_index("space") % 2 == 1
    moves, own = [], []
    for q in range(2):
        move = path[q][first : first + 2] - ends_ref[q, EXT : EXT + 2]
        moves.append(repeat_rows(move[:1], move[1:]))
        upper = lax.broadcasted_iota(jnp.int32, kept_ref.shape[1:], 0) >= CF
        own.append(shifted(jnp.where(upper == odd, kept_ref[q], end_ref[q]), CF, 0))
    lifted = by_pieces(jnp.concatenate(moves, axis=0), spread_ref[...])
    copies = []
    width = out_hbm.shape[2] // OUT_PIECES
    for i in range(OUT_PIECES):
        cols = slice(i * width, (i + 1) * width)
        for q in range(2):
            stage_ref[q, :, cols] = own[q][:, cols] + lifted[q * ROWS : (q + 1) * ROWS, cols]
        copy = pltpu.make_async_copy(stage_ref.at[:, :, cols], out_hbm.at[:, :, cols], sems.at[i])
        copy.start()
        copies.append(copy)
    for copy in copies:
        copy.wait()


def early_kernel(among, kept_ref, end_ref, ends_ref, spread_ref, *rest):
    held, (out_hbm, stage_ref, sems) = rest[:-3], rest[-3:]
    group = lax.axis_index("tm")

    @pl.when(group < among)
    def _():
        corrected(
            group, among, held, kept_ref, end_ref, ends_ref, spread_ref, out_hbm, stage_ref, sems
        )


def late_kernel(groups, among, before_hbm, kept_ref, end_ref, ends_ref, spread_ref, *rest):
    held, (out_hbm, stage_ref, sems) = rest[:-3], rest[-3:]
    group = lax.axis_index("tm")

    @pl.when(group >= among)
    def _():
        corrected(
            group, groups, held, kept_ref, end_ref, ends_ref, spread_ref, out_hbm, stage_ref, sems
        )


def call(kernel, shapes, operands, cost=0, hbm=(), smem=(), scratch=(), out=VMEM, alias=None):
    where = [VMEM] * len(operands)
    for i in hbm:
        where[i] = pl.BlockSpec(memory_space=pl.ANY)
    for i in smem:
        where[i] = pl.BlockSpec(memory_space=pltpu.SMEM)
    return pl.pallas_call(
        kernel,
        out_shape=[jax.ShapeDtypeStruct(shape, dtype) for shape, dtype in shapes],
        in_specs=where,
        out_specs=[out] * len(shapes),
        input_output_aliases=alias or {},
        scratch_shapes=scratch,
        cost_estimate=pl.CostEstimate(flops=cost, bytes_accessed=cost // 8, transcendentals=0),
        compiler_params=pltpu.CompilerParams(vmem_limit_bytes=16 * 1024 * 1024),
    )(*operands)


def hold():
    at = lax.axis_index("space") % 4
    turns = jnp.where((at == 1) | (at == 2), HOLD_TURNS, 0)
    return lax.fori_loop(0, turns, lambda i, x: x * 1664525 + 1013904223, at)


def from_near(block):
    pairs = [(i, i ^ 1) for i in range(lax.axis_size("space"))]
    return lax.ppermute(block, "space", pairs)


def from_far(block, step, among):
    count, groups = lax.axis_size("space"), lax.axis_size("tm")
    pairs = []
    for t in range(groups):
        for i in range(count):
            away = step if (i + step) % 2 == 0 else -step
            to = (i + away) % count if t < among else i ^ 1
            pairs.append((t * count + i, t * count + to))
    return lax.ppermute(block, ("tm", "space"), pairs)


def forward(groups, distance):
    pairs = [(i, (i + distance) % groups) for i in range(groups)]
    if distance == 2 and groups > 2:
        pairs[-2:] = [(groups - 2, 1), (groups - 1, 0)]
    return pairs


def step(c_state):
    own = c_state[0]
    rows, cols = own.shape[1:]
    count, groups = lax.axis_size("space"), lax.axis_size("tm")
    assert rows == HALO == ROWS and count % 2 == 0
    full, half = jnp.float32, jnp.bfloat16
    inner, wide = rows // CF, cols // CF
    reach, among = groups - 1, groups - 1 - EXT
    depth = -(-(reach - EXT) // inner)
    held_back = hold()
    far = from_far(own, 1, groups)
    near = from_near(own)
    farther = from_far(own, 2, among) if depth == 1 else None
    own_here, own_sums, gather, spread = call(
        ready_kernel,
        [
            (own.shape, full),
            ((ROWS, cols), full),
            ((CF * LANES, LANES), half),
            ((LANES, CF * LANES), half),
        ],
        (held_back.reshape(1), own),
        cost=4_000_000,
        hbm=(1,),
        smem=(0,),
        scratch=[pltpu.SemaphoreType.DMA],
    )
    edges = ((FSTEPS, *own.shape), full)
    tile = ((2, ROWS, wide), full)
    first, second, kept, near_start, near_end = call(
        near_kernel,
        [edges, edges, (own.shape, full), tile, tile],
        (near, own_here, own_sums, gather),
        cost=8_000_000,
    )
    sent_shape = (2, inner + 2 * EXT, wide)
    end, sent, ends, trail, far_means = call(
        far_kernel,
        [
            (own.shape, full),
            (sent_shape, full),
            tile,
            ((FSTEPS - 1, *own.shape), full),
            ((ROWS, wide), full),
        ],
        (far, first, second, near_start, near_end, gather),
        cost=2_000_000,
    )
    near_rows = from_near(sent)
    window = ((2, inner * (2 * depth + 1) + 2 * EXT, wide), full)
    if depth == 1:
        (window,) = call(
            functools.partial(outer_kernel, among),
            [window],
            (far, trail, farther, far_means, gather, sent, near_rows),
            cost=2_000_000,
        )
    else:
        pieces = [sent, near_rows, from_far(sent, 1, among)]
        for d in range(2, depth + 1):
            for sign in (1, -1):
                pairs = [(i, (i + sign * d) % count) for i in range(count)]
                pieces.append(lax.ppermute(sent, "space", pairs))
        (window,) = call(functools.partial(window_kernel, depth), [window], pieces)
    held = [sent]
    for k in range(1, groups):
        held.append(lax.ppermute(sent if k <= EXT else window, "tm", forward(groups, k)))
    whole = (own.shape, full)
    scratch = [pltpu.VMEM(own.shape, full), pltpu.SemaphoreType.DMA((OUT_PIECES,))]
    early = min(groups, 1 + EXT)
    (after,) = call(
        functools.partial(early_kernel, early),
        [whole],
        (kept, end, ends, spread, *held[:early]),
        cost=1_000_000,
        scratch=scratch,
        out=pl.BlockSpec(memory_space=pltpu.HBM),
    )
    if groups > early:
        (after,) = call(
            functools.partial(late_kernel, groups, early),
            [whole],
            (after, kept, end, ends, spread, *held),
            cost=1_000_000,
            hbm=(0,),
            scratch=scratch,
            out=pl.BlockSpec(memory_space=pltpu.HBM),
            alias={0: 0},
        )
    return after[None]


def solution(mesh):
    placed = (P("tm", None, "space", None),)
    return jax.shard_map(
        step, mesh=mesh, in_specs=placed, out_specs=P("tm", None, "space", None), check_vma=False
    )
```

```python
import functools

import jax
import jax.numpy as jnp
from jax import lax
from jax.experimental import pallas as pl
from jax.experimental.pallas import tpu as pltpu
from jax.sharding import PartitionSpec as P


FSTEPS = 4
CF = 4
COURANT = 0.06
DIFFUSION = 0.04
COARSE_COURANT = COURANT * FSTEPS / CF
COARSE_DIFFUSION = DIFFUSION * FSTEPS / (CF * CF)
EXT = 1
HALO = FSTEPS + CF * EXT
LANES = 128
VMEM = pl.BlockSpec(memory_space=pltpu.VMEM)
ROWS = 8
OUT_PIECES = 2
HOLD_TURNS = 80
BRANCHES = 4


def shifted(field, amount, axis):
    return pltpu.roll(field, amount % field.shape[axis], axis)


def advance(fields, courant, diffusion, pitch):
    u, v = fields
    along_u, along_v = courant * u, courant * v
    above = jnp.maximum(along_u, 0.0) + diffusion
    below = above - along_u
    left = jnp.maximum(along_v, 0.0) + diffusion
    right = left - along_v
    center = 1.0 - ((above + below) + (left + right))
    return [
        center * q
        + (above * shifted(q, pitch, 0) + below * shifted(q, -pitch, 0))
        + (left * shifted(q, 1, 1) + right * shifted(q, -1, 1))
        for q in fields
    ]


def exact_dot(field, weights):
    parts = []
    for part in range(3):
        piece = field.astype(jnp.bfloat16)
        parts.append(piece)
        if part < 2:
            field = field - piece.astype(jnp.float32)
    count = field.shape[0]
    done = jnp.dot(jnp.concatenate(parts, axis=0), weights, preferred_element_type=jnp.float32)
    return done[:count] + (done[count : 2 * count] + done[2 * count :])


def block_weights(shape, value):
    long = 0 if shape[0] > shape[1] else 1
    at = lax.broadcasted_iota(jnp.int32, shape, long)
    to = lax.broadcasted_iota(jnp.int32, shape, 1 - long)
    return jnp.where(at // CF == to, value, 0.0).astype(jnp.bfloat16)


def by_pieces(field, weights):
    width, count = weights.shape[0], field.shape[0]
    pieces = [field[:, at : at + width] for at in range(0, field.shape[1], width)]
    done = exact_dot(jnp.concatenate(pieces, axis=0), weights)
    return jnp.concatenate([done[i * count : (i + 1) * count] for i in range(len(pieces))], axis=1)


def packed_sums(tiles):
    packed = None
    for i, tile in enumerate(tiles):
        total = tile + shifted(tile, -1, 0)
        total = total + shifted(total, -2, 0)
        if packed is None:
            packed = total
        else:
            row = lax.broadcasted_iota(jnp.int32, tile.shape, 0)
            packed = jnp.where(row % CF == i, shifted(total, i, 0), packed)
    return packed


def place(base, tile, odd, moves):
    row = lax.broadcasted_iota(jnp.int32, base.shape, 0)
    for source, on_odd, on_even in moves:
        turned = pltpu.roll(tile, jnp.where(odd, (on_odd - source) % ROWS, (on_even - source) % ROWS), 0)
        base = jnp.where(row == jnp.where(odd, on_odd, on_even), turned, base)
    return base


def repeat_rows(first, second):
    cols = first.shape[1]
    row = lax.broadcasted_iota(jnp.int32, (ROWS, cols), 0)
    return jnp.where(
        row < CF, jnp.broadcast_to(first, (ROWS, cols)), jnp.broadcast_to(second, (ROWS, cols))
    )


def ready_kernel(held_ref, own_hbm, own_ref, sums_ref, gather_ref, spread_ref, sem):
    load = pltpu.make_async_copy(own_hbm, own_ref, sem)
    load.start()
    gather_ref[...] = block_weights(gather_ref.shape, 1.0 / (CF * CF))
    spread_ref[...] = block_weights(spread_ref.shape, 1.0)
    load.wait()
    sums_ref[...] = packed_sums([own_ref[0], own_ref[1]])


def near_kernel(
    near_ref, own_ref, sums_ref, gather_ref, first_ref, second_ref, kept_ref, start_ref, end_ref
):
    odd = lax.axis_index("space") % 2 == 1
    fields = []
    for q in range(2):
        near, own = near_ref[q], own_ref[q]
        low, high = jnp.where(odd, near, own), jnp.where(odd, own, near)
        fields.append(jnp.concatenate([low, high], axis=0))
    near_sums = packed_sums([near_ref[0], near_ref[1]])
    row = lax.broadcasted_iota(jnp.int32, near_sums.shape, 0)
    near_sums = jnp.where(row % CF < 2, near_sums, shifted(sums_ref[...], 2, 0))
    for k in range(1, FSTEPS + 1):
        for q in range(2):
            own = jnp.where(odd, fields[q][ROWS:], fields[q][:ROWS])
            first_ref[k - 1, q] = pltpu.roll(own, jnp.where(odd, k, ROWS - k), 0)
            second_ref[k - 1, q] = pltpu.roll(own, jnp.where(odd, k + 1, ROWS - 1 - k), 0)
        fields = advance(fields, COURANT, DIFFUSION, 1)
    kept = [shifted(q, -CF, 0)[:ROWS] for q in fields]
    for q in range(2):
        kept_ref[q] = kept[q]
    end_sums = packed_sums(kept)
    both = by_pieces(jnp.concatenate([near_sums, end_sums], axis=0), gather_ref[...])
    begun, ended = both[:ROWS], both[ROWS:]
    none = jnp.zeros_like(begun)
    for q in range(2):
        own = ((2 + q, 1, 1), (CF + 2 + q, 2, 2))
        start_ref[q] = place(none, begun, odd, ((q, 7, 3), (CF + q, 0, 4), *own))
        end_ref[q] = place(none, ended, odd, ((q, 0, 2), (CF + q, 1, 3)))


def slanted(outer, first, second, odd):
    sign = jnp.where(odd, 1.0, -1.0)
    turn = jnp.where(odd, 1, ROWS - 1)
    row = lax.broadcasted_iota(jnp.int32, outer[0].shape, 0)
    edge = row == jnp.where(odd, 0, ROWS - 1)
    fields = [jnp.where(edge, first[q], pltpu.roll(outer[q], turn, 0)) for q in range(2)]
    inner = [jnp.where(edge, second[q], pltpu.roll(fields[q], turn, 0)) for q in range(2)]
    along_u, along_v = (sign * COURANT) * fields[0], COURANT * fields[1]
    toward = jnp.maximum(along_u, 0.0) + DIFFUSION
    away = toward - along_u
    left = jnp.maximum(along_v, 0.0) + DIFFUSION
    right = left - along_v
    center = 1.0 - ((toward + away) + (left + right))
    return [
        center * fields[q]
        + (toward * inner[q] + away * outer[q])
        + (left * shifted(fields[q], 1, 1) + right * shifted(fields[q], -1, 1))
        for q in range(2)
    ]


def window_means(ends, starts, gather):
    packed = packed_sums(ends)
    row = lax.broadcasted_iota(jnp.int32, packed.shape, 0)
    packed = jnp.where(row % CF < 2, packed, shifted(packed_sums(starts), 2, 0))
    return by_pieces(packed, gather)


def passed_on(end, start, first_group):
    coarse = advance(start, COARSE_COURANT, COARSE_DIFFUSION, 1)
    defects = [end[q] - coarse[q] for q in range(2)]
    return [jnp.where(first_group, coarse[q] + defects[q], defects[q]) for q in range(2)]


def far_kernel(
    far_ref,
    first_ref,
    second_ref,
    near_start_ref,
    near_end_ref,
    gather_ref,
    end_ref,
    sent_ref,
    ends_ref,
    trail_ref,
    far_means_ref,
):
    odd = lax.axis_index("space") % 2 == 1
    first_group = lax.axis_index("tm") == 0
    fields = [far_ref[0], far_ref[1]]
    for k in range(FSTEPS):
        fields = slanted(fields, first_ref[k], second_ref[k], odd)
        if k < FSTEPS - 1:
            for q in range(2):
                trail_ref[k, q] = fields[q]
    for q in range(2):
        end_ref[q] = fields[q]
    far_means = window_means(fields, [far_ref[0], far_ref[1]], gather_ref[...])
    far_means_ref[...] = far_means
    start, end = [], []
    for q in range(2):
        moves = ((2 + q, 3, 7), (CF + 2 + q, 4, 0))
        start.append(place(near_start_ref[q], far_means, odd, moves))
        end.append(place(near_end_ref[q], far_means, odd, ((q, 2, 0), (CF + q, 3, 1))))
    sent = passed_on(end, start, first_group)
    for q in range(2):
        sent_ref[q] = sent[q][: 2 + 2 * EXT]
        ends_ref[q] = end[q]


def outer_kernel(
    among, far_ref, trail_ref, farther_ref, far_means_ref, gather_ref, sent_ref, near_ref, window_ref
):
    odd = lax.axis_index("space") % 2 == 1
    turn = jnp.where(odd, 1, ROWS - 1)
    group = lax.axis_index("tm")

    @pl.when(group >= among)
    def _():
        window_ref[...] = jnp.zeros_like(window_ref)

    @pl.when(group < among)
    def _():
        fields = [farther_ref[0], farther_ref[1]]
        for k in range(FSTEPS):
            beside = far_ref if k == 0 else trail_ref.at[k - 1]
            first = [pltpu.roll(beside[q], turn, 0) for q in range(2)]
            second = [pltpu.roll(first[q], turn, 0) for q in range(2)]
            fields = slanted(fields, first, second, odd)
        outer_means = window_means(fields, [farther_ref[0], farther_ref[1]], gather_ref[...])
        none = jnp.zeros((ROWS, outer_means.shape[1]), jnp.float32)
        gap = none[:2]
        start, end, window = [], [], []
        for q in range(2):
            begun = place(none, far_means_ref[...], odd, ((2 + q, 5, 1), (CF + 2 + q, 6, 2)))
            moves = ((2 + q, 7, 7), (CF + 2 + q, 0, 0))
            start.append(place(begun, outer_means, odd, moves))
            end.append(place(none, outer_means, odd, ((q, 6, 0), (CF + q, 7, 1))))
            beside = jnp.concatenate([near_ref[q], near_ref[q]], axis=0)
            middle = jnp.concatenate([gap, sent_ref[q], gap], axis=0)
            row = lax.broadcasted_iota(jnp.int32, none.shape, 0)
            window.append(jnp.where((row >= 2) & (row < 6), middle, beside))
        added = passed_on(end, start, group == 0)
        fresh = (row >= 6) == odd
        inside = (row >= 2) & (row < 6)
        for q in range(2):
            window_ref[q] = jnp.where(fresh & jnp.logical_not(inside), added[q], window[q])


def window_kernel(depth, own_ref, near_ref, far_ref, *rest):
    others, window_ref = rest[:-1], rest[-1]
    odd = lax.axis_index("space") % 2 == 1
    inner = own_ref.shape[1] - 2 * EXT
    for q in range(2):
        near, far = near_ref[q], far_ref[q]
        low, high = [jnp.where(odd, near, far)], [jnp.where(odd, far, near)]
        low += [others[2 * d][q] for d in range(depth - 1)]
        high += [others[2 * d + 1][q] for d in range(depth - 1)]
        parts = [low[-1][: EXT + inner]]
        parts += [part[EXT : EXT + inner] for part in reversed(low[:-1])]
        parts += [own_ref[q, EXT : EXT + inner]]
        parts += [part[EXT : EXT + inner] for part in high[:-1]]
        parts += [high[-1][EXT:]]
        window_ref[q] = jnp.concatenate(parts, axis=0)


def corrected(group, groups, held, kept_ref, end_ref, ends_ref, spread_ref, out_hbm, stage_ref, sems):
    reach = max(ref.shape[1] for ref in held)

    def placed(ref, q):
        term = ref[q]
        spare = (reach - term.shape[0]) // 2
        if spare:
            none = jnp.zeros((spare, term.shape[1]), jnp.float32)
            term = jnp.concatenate([none, term, none], axis=0)
        return term

    known = isinstance(group, int)
    terms = [[placed(ref, q) for q in range(2)] for ref in held[: group + 1 if known else None]]

    def of(index):
        if known:
            return terms[group - index]
        if index == groups - 1:
            return terms[0]
        picked = terms[min(len(terms) - 1, groups - 1 - index)]
        for k in range(min(len(terms) - 1, groups - 1 - index) - 1, -1, -1):
            picked = [jnp.where(group == index + k, terms[k][q], picked[q]) for q in range(2)]
        return picked

    path = of(0)
    for index in range(1, group + 1 if known else groups):
        term = of(index)
        after = advance(path, COARSE_COURANT, COARSE_DIFFUSION, 1)
        after = [after[q] + term[q] for q in range(2)]
        path = after if known else [jnp.where(index <= group, after[q], path[q]) for q in range(2)]
    first = (reach - 2) // 2
    odd = lax.axis_index("space") % 2 == 1
    moves, own = [], []
    for q in range(2):
        move = path[q][first : first + 2] - ends_ref[q, EXT : EXT + 2]
        moves.append(repeat_rows(move[:1], move[1:]))
        upper = lax.broadcasted_iota(jnp.int32, kept_ref.shape[1:], 0) >= CF
        own.append(shifted(jnp.where(upper == odd, kept_ref[q], end_ref[q]), CF, 0))
    lifted = by_pieces(jnp.concatenate(moves, axis=0), spread_ref[...])
    copies = []
    width = out_hbm.shape[2] // OUT_PIECES
    for i in range(OUT_PIECES):
        cols = slice(i * width, (i + 1) * width)
        for q in range(2):
            stage_ref[q, :, cols] = own[q][:, cols] + lifted[q * ROWS : (q + 1) * ROWS, cols]
        copy = pltpu.make_async_copy(stage_ref.at[:, :, cols], out_hbm.at[:, :, cols], sems.at[i])
        copy.start()
        copies.append(copy)
    for copy in copies:
        copy.wait()


def by_group(first, last, *refs):
    group = lax.axis_index("tm")
    if last <= BRANCHES:
        for g in range(first, last):
            pl.when(group == g)(functools.partial(corrected, g, last, *refs))
    else:
        inside = (group >= first) & (group < last)
        pl.when(inside)(functools.partial(corrected, group, last, *refs))


def early_kernel(among, kept_ref, end_ref, ends_ref, spread_ref, *rest):
    held, (out_hbm, stage_ref, sems) = rest[:-3], rest[-3:]
    by_group(0, among, held, kept_ref, end_ref, ends_ref, spread_ref, out_hbm, stage_ref, sems)


def late_kernel(groups, among, before_hbm, kept_ref, end_ref, ends_ref, spread_ref, *rest):
    held, (out_hbm, stage_ref, sems) = rest[:-3], rest[-3:]
    by_group(among, groups, held, kept_ref, end_ref, ends_ref, spread_ref, out_hbm, stage_ref, sems)


def call(kernel, shapes, operands, cost=0, hbm=(), smem=(), scratch=(), out=VMEM, alias=None):
    where = [VMEM] * len(operands)
    for i in hbm:
        where[i] = pl.BlockSpec(memory_space=pl.ANY)
    for i in smem:
        where[i] = pl.BlockSpec(memory_space=pltpu.SMEM)
    return pl.pallas_call(
        kernel,
        out_shape=[jax.ShapeDtypeStruct(shape, dtype) for shape, dtype in shapes],
        in_specs=where,
        out_specs=[out] * len(shapes),
        input_output_aliases=alias or {},
        scratch_shapes=scratch,
        cost_estimate=pl.CostEstimate(flops=cost, bytes_accessed=cost // 8, transcendentals=0),
        compiler_params=pltpu.CompilerParams(vmem_limit_bytes=16 * 1024 * 1024),
    )(*operands)


def hold():
    at = lax.axis_index("space") % 4
    turns = jnp.where((at == 1) | (at == 2), HOLD_TURNS, 0)
    return lax.fori_loop(0, turns, lambda i, x: x * 1664525 + 1013904223, at)


def from_near(block):
    pairs = [(i, i ^ 1) for i in range(lax.axis_size("space"))]
    return lax.ppermute(block, "space", pairs)


def from_far(block, step, among):
    count, groups = lax.axis_size("space"), lax.axis_size("tm")
    pairs = []
    for t in range(groups):
        for i in range(count):
            away = step if (i + step) % 2 == 0 else -step
            to = (i + away) % count if t < among else i ^ 1
            pairs.append((t * count + i, t * count + to))
    return lax.ppermute(block, ("tm", "space"), pairs)


def forward(groups, distance):
    pairs = [(i, (i + distance) % groups) for i in range(groups)]
    if distance == 2 and groups > 2:
        pairs[-2:] = [(groups - 2, 1), (groups - 1, 0)]
    return pairs


def step(c_state):
    own = c_state[0]
    rows, cols = own.shape[1:]
    count, groups = lax.axis_size("space"), lax.axis_size("tm")
    assert rows == HALO == ROWS and count % 2 == 0
    full, half = jnp.float32, jnp.bfloat16
    inner, wide = rows // CF, cols // CF
    reach, among = groups - 1, groups - 1 - EXT
    depth = -(-(reach - EXT) // inner)
    held_back = hold()
    far = from_far(own, 1, groups)
    near = from_near(own)
    farther = from_far(own, 2, among) if depth == 1 else None
    own_here, own_sums, gather, spread = call(
        ready_kernel,
        [
            (own.shape, full),
            ((ROWS, cols), full),
            ((CF * LANES, LANES), half),
            ((LANES, CF * LANES), half),
        ],
        (held_back.reshape(1), own),
        cost=4_000_000,
        hbm=(1,),
        smem=(0,),
        scratch=[pltpu.SemaphoreType.DMA],
    )
    edges = ((FSTEPS, *own.shape), full)
    tile = ((2, ROWS, wide), full)
    first, second, kept, near_start, near_end = call(
        near_kernel,
        [edges, edges, (own.shape, full), tile, tile],
        (near, own_here, own_sums, gather),
        cost=8_000_000,
    )
    sent_shape = (2, inner + 2 * EXT, wide)
    end, sent, ends, trail, far_means = call(
        far_kernel,
        [
            (own.shape, full),
            (sent_shape, full),
            tile,
            ((FSTEPS - 1, *own.shape), full),
            ((ROWS, wide), full),
        ],
        (far, first, second, near_start, near_end, gather),
        cost=2_000_000,
    )
    near_rows = from_near(sent)
    window = ((2, inner * (2 * depth + 1) + 2 * EXT, wide), full)
    if depth == 1:
        (window,) = call(
            functools.partial(outer_kernel, among),
            [window],
            (far, trail, farther, far_means, gather, sent, near_rows),
            cost=2_000_000,
        )
    else:
        pieces = [sent, near_rows, from_far(sent, 1, among)]
        for d in range(2, depth + 1):
            for sign in (1, -1):
                pairs = [(i, (i + sign * d) % count) for i in range(count)]
                pieces.append(lax.ppermute(sent, "space", pairs))
        (window,) = call(functools.partial(window_kernel, depth), [window], pieces)
    held = [sent]
    for k in range(1, groups):
        held.append(lax.ppermute(sent if k <= EXT else window, "tm", forward(groups, k)))
    whole = (own.shape, full)
    scratch = [pltpu.VMEM(own.shape, full), pltpu.SemaphoreType.DMA((OUT_PIECES,))]
    early = min(groups, 1 + EXT)
    (after,) = call(
        functools.partial(early_kernel, early),
        [whole],
        (kept, end, ends, spread, *held[:early]),
        cost=1_000_000,
        scratch=scratch,
        out=pl.BlockSpec(memory_space=pltpu.HBM),
    )
    if groups > early:
        (after,) = call(
            functools.partial(late_kernel, groups, early),
            [whole],
            (after, kept, end, ends, spread, *held),
            cost=1_000_000,
            hbm=(0,),
            scratch=scratch,
            out=pl.BlockSpec(memory_space=pltpu.HBM),
            alias={0: 0},
        )
    return after[None]


def solution(mesh):
    placed = (P("tm", None, "space", None),)
    return jax.shard_map(
        step, mesh=mesh, in_specs=placed, out_specs=P("tm", None, "space", None), check_vma=False
    )
```

```python
import functools

import jax
import jax.numpy as jnp
from jax import lax
from jax.experimental import pallas as pl
from jax.experimental.pallas import tpu as pltpu
from jax.sharding import PartitionSpec as P


FSTEPS = 4
CF = 4
COURANT = 0.06
DIFFUSION = 0.04
COARSE_COURANT = COURANT * FSTEPS / CF
COARSE_DIFFUSION = DIFFUSION * FSTEPS / (CF * CF)
EXT = 1
HALO = FSTEPS + CF * EXT
LANES = 128
VMEM = pl.BlockSpec(memory_space=pltpu.VMEM)
ROWS = 8
OUT_PIECES = 2
HOLD_TURNS = 80
BRANCHES = 4


def shifted(field, amount, axis):
    return pltpu.roll(field, amount % field.shape[axis], axis)


def advance(fields, courant, diffusion, pitch):
    u, v = fields
    along_u, along_v = courant * u, courant * v
    above = jnp.maximum(along_u, 0.0) + diffusion
    below = above - along_u
    left = jnp.maximum(along_v, 0.0) + diffusion
    right = left - along_v
    center = 1.0 - ((above + below) + (left + right))
    return [
        center * q
        + (above * shifted(q, pitch, 0) + below * shifted(q, -pitch, 0))
        + (left * shifted(q, 1, 1) + right * shifted(q, -1, 1))
        for q in fields
    ]


def exact_dot(field, weights):
    parts = []
    for part in range(3):
        piece = field.astype(jnp.bfloat16)
        parts.append(piece)
        if part < 2:
            field = field - piece.astype(jnp.float32)
    count = field.shape[0]
    done = jnp.dot(jnp.concatenate(parts, axis=0), weights, preferred_element_type=jnp.float32)
    return done[:count] + (done[count : 2 * count] + done[2 * count :])


def block_weights(shape, value):
    long = 0 if shape[0] > shape[1] else 1
    at = lax.broadcasted_iota(jnp.int32, shape, long)
    to = lax.broadcasted_iota(jnp.int32, shape, 1 - long)
    return jnp.where(at // CF == to, value, 0.0).astype(jnp.bfloat16)


def by_pieces(field, weights):
    width, count = weights.shape[0], field.shape[0]
    pieces = [field[:, at : at + width] for at in range(0, field.shape[1], width)]
    done = exact_dot(jnp.concatenate(pieces, axis=0), weights)
    return jnp.concatenate([done[i * count : (i + 1) * count] for i in range(len(pieces))], axis=1)


def packed_sums(tiles):
    packed = None
    for i, tile in enumerate(tiles):
        total = tile + shifted(tile, -1, 0)
        total = total + shifted(total, -2, 0)
        if packed is None:
            packed = total
        else:
            row = lax.broadcasted_iota(jnp.int32, tile.shape, 0)
            packed = jnp.where(row % CF == i, shifted(total, i, 0), packed)
    return packed


def place(base, tile, odd, moves):
    row = lax.broadcasted_iota(jnp.int32, base.shape, 0)
    for source, on_odd, on_even in moves:
        turned = pltpu.roll(tile, jnp.where(odd, (on_odd - source) % ROWS, (on_even - source) % ROWS), 0)
        base = jnp.where(row == jnp.where(odd, on_odd, on_even), turned, base)
    return base


def repeat_rows(first, second):
    cols = first.shape[1]
    row = lax.broadcasted_iota(jnp.int32, (ROWS, cols), 0)
    return jnp.where(
        row < CF, jnp.broadcast_to(first, (ROWS, cols)), jnp.broadcast_to(second, (ROWS, cols))
    )


def ready_kernel(held_ref, own_hbm, own_ref, sums_ref, gather_ref, spread_ref, sem):
    load = pltpu.make_async_copy(own_hbm, own_ref, sem)
    load.start()
    gather_ref[...] = block_weights(gather_ref.shape, 1.0 / (CF * CF))
    spread_ref[...] = block_weights(spread_ref.shape, 1.0)
    load.wait()
    sums_ref[...] = packed_sums([own_ref[0], own_ref[1]])


def near_kernel(
    near_ref, own_ref, sums_ref, gather_ref, first_ref, second_ref, kept_ref, start_ref, end_ref
):
    odd = lax.axis_index("space") % 2 == 1
    fields = []
    for q in range(2):
        near, own = near_ref[q], own_ref[q]
        low, high = jnp.where(odd, near, own), jnp.where(odd, own, near)
        fields.append(jnp.concatenate([low, high], axis=0))
    near_sums = packed_sums([near_ref[0], near_ref[1]])
    row = lax.broadcasted_iota(jnp.int32, near_sums.shape, 0)
    near_sums = jnp.where(row % CF < 2, near_sums, shifted(sums_ref[...], 2, 0))
    for k in range(1, FSTEPS + 1):
        for q in range(2):
            own = jnp.where(odd, fields[q][ROWS:], fields[q][:ROWS])
            first_ref[k - 1, q] = pltpu.roll(own, jnp.where(odd, k, ROWS - k), 0)
            second_ref[k - 1, q] = pltpu.roll(own, jnp.where(odd, k + 1, ROWS - 1 - k), 0)
        fields = advance(fields, COURANT, DIFFUSION, 1)
    kept = [shifted(q, -CF, 0)[:ROWS] for q in fields]
    for q in range(2):
        kept_ref[q] = kept[q]
    end_sums = packed_sums(kept)
    both = by_pieces(jnp.concatenate([near_sums, end_sums], axis=0), gather_ref[...])
    begun, ended = both[:ROWS], both[ROWS:]
    none = jnp.zeros_like(begun)
    for q in range(2):
        own = ((2 + q, 1, 1), (CF + 2 + q, 2, 2))
        start_ref[q] = place(none, begun, odd, ((q, 7, 3), (CF + q, 0, 4), *own))
        end_ref[q] = place(none, ended, odd, ((q, 0, 2), (CF + q, 1, 3)))


def slanted(outer, first, second, odd):
    sign = jnp.where(odd, 1.0, -1.0)
    turn = jnp.where(odd, 1, ROWS - 1)
    row = lax.broadcasted_iota(jnp.int32, outer[0].shape, 0)
    edge = row == jnp.where(odd, 0, ROWS - 1)
    fields = [jnp.where(edge, first[q], pltpu.roll(outer[q], turn, 0)) for q in range(2)]
    inner = [jnp.where(edge, second[q], pltpu.roll(fields[q], turn, 0)) for q in range(2)]
    along_u, along_v = (sign * COURANT) * fields[0], COURANT * fields[1]
    toward = jnp.maximum(along_u, 0.0) + DIFFUSION
    away = toward - along_u
    left = jnp.maximum(along_v, 0.0) + DIFFUSION
    right = left - along_v
    center = 1.0 - ((toward + away) + (left + right))
    return [
        center * fields[q]
        + (toward * inner[q] + away * outer[q])
        + (left * shifted(fields[q], 1, 1) + right * shifted(fields[q], -1, 1))
        for q in range(2)
    ]


def window_means(ends, starts, gather):
    packed = packed_sums(ends)
    row = lax.broadcasted_iota(jnp.int32, packed.shape, 0)
    packed = jnp.where(row % CF < 2, packed, shifted(packed_sums(starts), 2, 0))
    return by_pieces(packed, gather)


def passed_on(end, start, first_group):
    coarse = advance(start, COARSE_COURANT, COARSE_DIFFUSION, 1)
    defects = [end[q] - coarse[q] for q in range(2)]
    return [jnp.where(first_group, coarse[q] + defects[q], defects[q]) for q in range(2)]


def far_kernel(
    far_ref,
    first_ref,
    second_ref,
    near_start_ref,
    near_end_ref,
    gather_ref,
    end_ref,
    sent_ref,
    ends_ref,
    trail_ref,
    far_means_ref,
):
    odd = lax.axis_index("space") % 2 == 1
    first_group = lax.axis_index("tm") == 0
    fields = [far_ref[0], far_ref[1]]
    for k in range(FSTEPS):
        fields = slanted(fields, first_ref[k], second_ref[k], odd)
        if k < FSTEPS - 1:
            for q in range(2):
                trail_ref[k, q] = fields[q]
    for q in range(2):
        end_ref[q] = fields[q]
    far_means = window_means(fields, [far_ref[0], far_ref[1]], gather_ref[...])
    far_means_ref[...] = far_means
    start, end = [], []
    for q in range(2):
        moves = ((2 + q, 3, 7), (CF + 2 + q, 4, 0))
        start.append(place(near_start_ref[q], far_means, odd, moves))
        end.append(place(near_end_ref[q], far_means, odd, ((q, 2, 0), (CF + q, 3, 1))))
    sent = passed_on(end, start, first_group)
    for q in range(2):
        sent_ref[q] = sent[q][: 2 + 2 * EXT]
        ends_ref[q] = end[q]


def outer_kernel(
    among, far_ref, trail_ref, farther_ref, far_means_ref, gather_ref, sent_ref, near_ref, window_ref
):
    odd = lax.axis_index("space") % 2 == 1
    turn = jnp.where(odd, 1, ROWS - 1)
    group = lax.axis_index("tm")

    @pl.when(group >= among)
    def _():
        window_ref[...] = jnp.zeros_like(window_ref)

    @pl.when(group < among)
    def _():
        fields = [farther_ref[0], farther_ref[1]]
        for k in range(FSTEPS):
            beside = far_ref if k == 0 else trail_ref.at[k - 1]
            first = [pltpu.roll(beside[q], turn, 0) for q in range(2)]
            second = [pltpu.roll(first[q], turn, 0) for q in range(2)]
            fields = slanted(fields, first, second, odd)
        outer_means = window_means(fields, [farther_ref[0], farther_ref[1]], gather_ref[...])
        none = jnp.zeros((ROWS, outer_means.shape[1]), jnp.float32)
        gap = none[:2]
        start, end, window = [], [], []
        for q in range(2):
            begun = place(none, far_means_ref[...], odd, ((2 + q, 5, 1), (CF + 2 + q, 6, 2)))
            moves = ((2 + q, 7, 7), (CF + 2 + q, 0, 0))
            start.append(place(begun, outer_means, odd, moves))
            end.append(place(none, outer_means, odd, ((q, 6, 0), (CF + q, 7, 1))))
            beside = jnp.concatenate([near_ref[q], near_ref[q]], axis=0)
            middle = jnp.concatenate([gap, sent_ref[q], gap], axis=0)
            row = lax.broadcasted_iota(jnp.int32, none.shape, 0)
            window.append(jnp.where((row >= 2) & (row < 6), middle, beside))
        added = passed_on(end, start, group == 0)
        fresh = (row >= 6) == odd
        inside = (row >= 2) & (row < 6)
        for q in range(2):
            window_ref[q] = jnp.where(fresh & jnp.logical_not(inside), added[q], window[q])


def window_kernel(depth, own_ref, near_ref, far_ref, *rest):
    others, window_ref = rest[:-1], rest[-1]
    odd = lax.axis_index("space") % 2 == 1
    inner = own_ref.shape[1] - 2 * EXT
    for q in range(2):
        near, far = near_ref[q], far_ref[q]
        low, high = [jnp.where(odd, near, far)], [jnp.where(odd, far, near)]
        low += [others[2 * d][q] for d in range(depth - 1)]
        high += [others[2 * d + 1][q] for d in range(depth - 1)]
        parts = [low[-1][: EXT + inner]]
        parts += [part[EXT : EXT + inner] for part in reversed(low[:-1])]
        parts += [own_ref[q, EXT : EXT + inner]]
        parts += [part[EXT : EXT + inner] for part in high[:-1]]
        parts += [high[-1][EXT:]]
        window_ref[q] = jnp.concatenate(parts, axis=0)


def corrected(group, groups, held, kept_ref, end_ref, ends_ref, spread_ref, out_hbm, stage_ref, sems):
    reach = max(ref.shape[1] for ref in held)

    def placed(ref, q):
        term = ref[q]
        spare = (reach - term.shape[0]) // 2
        if spare:
            none = jnp.zeros((spare, term.shape[1]), jnp.float32)
            term = jnp.concatenate([none, term, none], axis=0)
        return term

    known = isinstance(group, int)
    terms = [[placed(ref, q) for q in range(2)] for ref in held[: group + 1 if known else None]]

    def of(index):
        if known:
            return terms[group - index]
        if index == groups - 1:
            return terms[0]
        picked = terms[min(len(terms) - 1, groups - 1 - index)]
        for k in range(min(len(terms) - 1, groups - 1 - index) - 1, -1, -1):
            picked = [jnp.where(group == index + k, terms[k][q], picked[q]) for q in range(2)]
        return picked

    path = of(0)
    for index in range(1, group + 1 if known else groups):
        term = of(index)
        after = advance(path, COARSE_COURANT, COARSE_DIFFUSION, 1)
        after = [after[q] + term[q] for q in range(2)]
        path = after if known else [jnp.where(index <= group, after[q], path[q]) for q in range(2)]
    first = (reach - 2) // 2
    odd = lax.axis_index("space") % 2 == 1
    moves, own = [], []
    for q in range(2):
        move = path[q][first : first + 2] - ends_ref[q, EXT : EXT + 2]
        moves.append(repeat_rows(move[:1], move[1:]))
        upper = lax.broadcasted_iota(jnp.int32, kept_ref.shape[1:], 0) >= CF
        own.append(shifted(jnp.where(upper == odd, kept_ref[q], end_ref[q]), CF, 0))
    lifted = by_pieces(jnp.concatenate(moves, axis=0), spread_ref[...])
    copies = []
    width = out_hbm.shape[2] // OUT_PIECES
    for i in range(OUT_PIECES):
        cols = slice(i * width, (i + 1) * width)
        for q in range(2):
            stage_ref[q, :, cols] = own[q][:, cols] + lifted[q * ROWS : (q + 1) * ROWS, cols]
        copy = pltpu.make_async_copy(stage_ref.at[:, :, cols], out_hbm.at[:, :, cols], sems.at[i])
        copy.start()
        copies.append(copy)
    for copy in copies:
        copy.wait()


def by_group(first, last, *refs):
    group = lax.axis_index("tm")
    if last <= BRANCHES:
        for g in range(first, last):
            pl.when(group == g)(functools.partial(corrected, g, last, *refs))
    else:
        inside = (group >= first) & (group < last)
        pl.when(inside)(functools.partial(corrected, group, last, *refs))


def early_kernel(among, kept_ref, end_ref, ends_ref, spread_ref, *rest):
    held, (out_hbm, stage_ref, sems) = rest[:-3], rest[-3:]
    by_group(0, among, held, kept_ref, end_ref, ends_ref, spread_ref, out_hbm, stage_ref, sems)


def late_kernel(groups, among, before_hbm, kept_ref, end_ref, ends_ref, spread_ref, *rest):
    held, (out_hbm, stage_ref, sems) = rest[:-3], rest[-3:]
    by_group(among, groups, held, kept_ref, end_ref, ends_ref, spread_ref, out_hbm, stage_ref, sems)


def call(kernel, shapes, operands, cost=0, hbm=(), smem=(), scratch=(), out=VMEM, alias=None):
    where = [VMEM] * len(operands)
    for i in hbm:
        where[i] = pl.BlockSpec(memory_space=pl.ANY)
    for i in smem:
        where[i] = pl.BlockSpec(memory_space=pltpu.SMEM)
    return pl.pallas_call(
        kernel,
        out_shape=[jax.ShapeDtypeStruct(shape, dtype) for shape, dtype in shapes],
        in_specs=where,
        out_specs=[out] * len(shapes),
        input_output_aliases=alias or {},
        scratch_shapes=scratch,
        cost_estimate=pl.CostEstimate(flops=cost, bytes_accessed=cost // 8, transcendentals=0),
        compiler_params=pltpu.CompilerParams(vmem_limit_bytes=16 * 1024 * 1024),
    )(*operands)


def moved(block, axis, pairs):
    return lax.ppermute(block, axis, pairs)


def hold():
    at = lax.axis_index("space") % 4
    turns = jnp.where((at == 1) | (at == 2), HOLD_TURNS, 0)
    return lax.fori_loop(0, turns, lambda i, x: x * 1664525 + 1013904223, at)


def from_near(block):
    pairs = [(i, i ^ 1) for i in range(lax.axis_size("space"))]
    return moved(block, "space", pairs)


def from_far(block, step, among):
    count, groups = lax.axis_size("space"), lax.axis_size("tm")
    pairs = []
    for t in range(groups):
        for i in range(count):
            away = step if (i + step) % 2 == 0 else -step
            to = (i + away) % count if t < among else i ^ 1
            pairs.append((t * count + i, t * count + to))
    return moved(block, ("tm", "space"), pairs)


def forward(groups, count, distance):
    later = [(i + distance) % groups for i in range(groups)]
    if distance == 2 and groups > 2:
        later[-2:] = [1, 0]
    aside = 1 if 2 < distance == groups - 1 else -1
    return [
        (i * count + s, later[i] * count + (s ^ 1 if i == aside else s))
        for i in range(groups)
        for s in range(count)
    ]


def step(c_state):
    own = c_state[0]
    rows, cols = own.shape[1:]
    count, groups = lax.axis_size("space"), lax.axis_size("tm")
    assert rows == HALO == ROWS and count % 2 == 0
    full, half = jnp.float32, jnp.bfloat16
    inner, wide = rows // CF, cols // CF
    reach, among = groups - 1, groups - 1 - EXT
    depth = -(-(reach - EXT) // inner)
    held_back = hold()
    far = from_far(own, 1, groups)
    near = from_near(own)
    farther = from_far(own, 2, among) if depth == 1 else None
    own_here, own_sums, gather, spread = call(
        ready_kernel,
        [
            (own.shape, full),
            ((ROWS, cols), full),
            ((CF * LANES, LANES), half),
            ((LANES, CF * LANES), half),
        ],
        (held_back.reshape(1), own),
        cost=4_000_000,
        hbm=(1,),
        smem=(0,),
        scratch=[pltpu.SemaphoreType.DMA],
    )
    edges = ((FSTEPS, *own.shape), full)
    tile = ((2, ROWS, wide), full)
    first, second, kept, near_start, near_end = call(
        near_kernel,
        [edges, edges, (own.shape, full), tile, tile],
        (near, own_here, own_sums, gather),
        cost=8_000_000,
    )
    sent_shape = (2, inner + 2 * EXT, wide)
    end, sent, ends, trail, far_means = call(
        far_kernel,
        [
            (own.shape, full),
            (sent_shape, full),
            tile,
            ((FSTEPS - 1, *own.shape), full),
            ((ROWS, wide), full),
        ],
        (far, first, second, near_start, near_end, gather),
        cost=2_000_000,
    )
    near_rows = from_near(sent)
    window = ((2, inner * (2 * depth + 1) + 2 * EXT, wide), full)
    if depth == 1:
        (window,) = call(
            functools.partial(outer_kernel, among),
            [window],
            (far, trail, farther, far_means, gather, sent, near_rows),
            cost=2_000_000,
        )
    else:
        pieces = [sent, near_rows, from_far(sent, 1, among)]
        for d in range(2, depth + 1):
            for sign in (1, -1):
                pairs = [(i, (i + sign * d) % count) for i in range(count)]
                pieces.append(lax.ppermute(sent, "space", pairs))
        (window,) = call(functools.partial(window_kernel, depth), [window], pieces)
    held = [sent]
    for k in range(1, groups):
        held.append(moved(sent if k <= EXT else window, ("tm", "space"), forward(groups, count, k)))
    whole = (own.shape, full)
    scratch = [pltpu.VMEM(own.shape, full), pltpu.SemaphoreType.DMA((OUT_PIECES,))]
    early = min(groups, 1 + EXT)
    (after,) = call(
        functools.partial(early_kernel, early),
        [whole],
        (kept, end, ends, spread, *held[:early]),
        cost=1_000_000,
        scratch=scratch,
        out=pl.BlockSpec(memory_space=pltpu.HBM),
    )
    if groups > early:
        (after,) = call(
            functools.partial(late_kernel, groups, early),
            [whole],
            (after, kept, end, ends, spread, *held),
            cost=1_000_000,
            hbm=(0,),
            scratch=scratch,
            out=pl.BlockSpec(memory_space=pltpu.HBM),
            alias={0: 0},
        )
    return after[None]


def solution(mesh):
    placed = (P("tm", None, "space", None),)
    return jax.shard_map(
        step, mesh=mesh, in_specs=placed, out_specs=P("tm", None, "space", None), check_vma=False
    )
```

```python
import functools

import jax
import jax.numpy as jnp
from jax import lax
from jax.experimental import pallas as pl
from jax.experimental.pallas import tpu as pltpu
from jax.sharding import PartitionSpec as P


FSTEPS = 4
CF = 4
COURANT = 0.06
DIFFUSION = 0.04
COARSE_COURANT = COURANT * FSTEPS / CF
COARSE_DIFFUSION = DIFFUSION * FSTEPS / (CF * CF)
EXT = 1
HALO = FSTEPS + CF * EXT
LANES = 128
VMEM = pl.BlockSpec(memory_space=pltpu.VMEM)
ROWS = 8
OUT_PIECES = 1
HOLD_TURNS = 80


def shifted(field, amount, axis):
    return pltpu.roll(field, amount % field.shape[axis], axis)


def advance(fields, courant, diffusion, pitch):
    u, v = fields
    along_u, along_v = courant * u, courant * v
    above = jnp.maximum(along_u, 0.0) + diffusion
    below = above - along_u
    left = jnp.maximum(along_v, 0.0) + diffusion
    right = left - along_v
    center = 1.0 - ((above + below) + (left + right))
    return [
        center * q
        + (above * shifted(q, pitch, 0) + below * shifted(q, -pitch, 0))
        + (left * shifted(q, 1, 1) + right * shifted(q, -1, 1))
        for q in fields
    ]


def exact_dot(field, weights):
    parts = []
    for part in range(3):
        piece = field.astype(jnp.bfloat16)
        parts.append(piece)
        if part < 2:
            field = field - piece.astype(jnp.float32)
    count = field.shape[0]
    done = jnp.dot(jnp.concatenate(parts, axis=0), weights, preferred_element_type=jnp.float32)
    return done[:count] + (done[count : 2 * count] + done[2 * count :])


def block_weights(shape, value):
    long = 0 if shape[0] > shape[1] else 1
    at = lax.broadcasted_iota(jnp.int32, shape, long)
    to = lax.broadcasted_iota(jnp.int32, shape, 1 - long)
    return jnp.where(at // CF == to, value, 0.0).astype(jnp.bfloat16)


def by_pieces(field, weights):
    width, count = weights.shape[0], field.shape[0]
    pieces = [field[:, at : at + width] for at in range(0, field.shape[1], width)]
    done = exact_dot(jnp.concatenate(pieces, axis=0), weights)
    return jnp.concatenate([done[i * count : (i + 1) * count] for i in range(len(pieces))], axis=1)


def packed_sums(tiles):
    packed = None
    for i, tile in enumerate(tiles):
        total = tile + shifted(tile, -1, 0)
        total = total + shifted(total, -2, 0)
        if packed is None:
            packed = total
        else:
            row = lax.broadcasted_iota(jnp.int32, tile.shape, 0)
            packed = jnp.where(row % CF == i, shifted(total, i, 0), packed)
    return packed


def place(base, tile, odd, moves):
    row = lax.broadcasted_iota(jnp.int32, base.shape, 0)
    for source, on_odd, on_even in moves:
        turned = pltpu.roll(tile, jnp.where(odd, (on_odd - source) % ROWS, (on_even - source) % ROWS), 0)
        base = jnp.where(row == jnp.where(odd, on_odd, on_even), turned, base)
    return base


def repeat_rows(first, second):
    cols = first.shape[1]
    row = lax.broadcasted_iota(jnp.int32, (ROWS, cols), 0)
    return jnp.where(
        row < CF, jnp.broadcast_to(first, (ROWS, cols)), jnp.broadcast_to(second, (ROWS, cols))
    )


def ready_kernel(held_ref, own_hbm, own_ref, sums_ref, gather_ref, spread_ref, sem):
    load = pltpu.make_async_copy(own_hbm, own_ref, sem)
    load.start()
    gather_ref[...] = block_weights(gather_ref.shape, 1.0 / (CF * CF))
    spread_ref[...] = block_weights(spread_ref.shape, 1.0)
    load.wait()
    sums_ref[...] = packed_sums([own_ref[0], own_ref[1]])


def near_kernel(
    near_ref, own_ref, sums_ref, gather_ref, first_ref, second_ref, kept_ref, start_ref, end_ref
):
    odd = lax.axis_index("space") % 2 == 1
    fields = []
    for q in range(2):
        near, own = near_ref[q], own_ref[q]
        low, high = jnp.where(odd, near, own), jnp.where(odd, own, near)
        fields.append(jnp.concatenate([low, high], axis=0))
    near_sums = packed_sums([near_ref[0], near_ref[1]])
    row = lax.broadcasted_iota(jnp.int32, near_sums.shape, 0)
    near_sums = jnp.where(row % CF < 2, near_sums, shifted(sums_ref[...], 2, 0))
    for k in range(1, FSTEPS + 1):
        for q in range(2):
            own = jnp.where(odd, fields[q][ROWS:], fields[q][:ROWS])
            first_ref[k - 1, q] = pltpu.roll(own, jnp.where(odd, k, ROWS - k), 0)
            second_ref[k - 1, q] = pltpu.roll(own, jnp.where(odd, k + 1, ROWS - 1 - k), 0)
        fields = advance(fields, COURANT, DIFFUSION, 1)
    kept = [shifted(q, -CF, 0)[:ROWS] for q in fields]
    for q in range(2):
        kept_ref[q] = kept[q]
    end_sums = packed_sums(kept)
    both = by_pieces(jnp.concatenate([near_sums, end_sums], axis=0), gather_ref[...])
    begun, ended = both[:ROWS], both[ROWS:]
    none = jnp.zeros_like(begun)
    for q in range(2):
        own = ((2 + q, 1, 1), (CF + 2 + q, 2, 2))
        start_ref[q] = place(none, begun, odd, ((q, 7, 3), (CF + q, 0, 4), *own))
        end_ref[q] = place(none, ended, odd, ((q, 0, 2), (CF + q, 1, 3)))


def slanted(outer, first, second, odd):
    sign = jnp.where(odd, 1.0, -1.0)
    turn = jnp.where(odd, 1, ROWS - 1)
    row = lax.broadcasted_iota(jnp.int32, outer[0].shape, 0)
    edge = row == jnp.where(odd, 0, ROWS - 1)
    fields = [jnp.where(edge, first[q], pltpu.roll(outer[q], turn, 0)) for q in range(2)]
    inner = [jnp.where(edge, second[q], pltpu.roll(fields[q], turn, 0)) for q in range(2)]
    along_u, along_v = (sign * COURANT) * fields[0], COURANT * fields[1]
    toward = jnp.maximum(along_u, 0.0) + DIFFUSION
    away = toward - along_u
    left = jnp.maximum(along_v, 0.0) + DIFFUSION
    right = left - along_v
    center = 1.0 - ((toward + away) + (left + right))
    return [
        center * fields[q]
        + (toward * inner[q] + away * outer[q])
        + (left * shifted(fields[q], 1, 1) + right * shifted(fields[q], -1, 1))
        for q in range(2)
    ]


def window_means(ends, starts, gather):
    packed = packed_sums(ends)
    row = lax.broadcasted_iota(jnp.int32, packed.shape, 0)
    packed = jnp.where(row % CF < 2, packed, shifted(packed_sums(starts), 2, 0))
    return by_pieces(packed, gather)


def passed_on(end, start, first_group):
    coarse = advance(start, COARSE_COURANT, COARSE_DIFFUSION, 1)
    defects = [end[q] - coarse[q] for q in range(2)]
    return [jnp.where(first_group, coarse[q] + defects[q], defects[q]) for q in range(2)]


def far_kernel(
    far_ref,
    first_ref,
    second_ref,
    near_start_ref,
    near_end_ref,
    gather_ref,
    end_ref,
    sent_ref,
    ends_ref,
    trail_ref,
    far_means_ref,
):
    odd = lax.axis_index("space") % 2 == 1
    first_group = lax.axis_index("tm") == 0
    fields = [far_ref[0], far_ref[1]]
    for k in range(FSTEPS):
        fields = slanted(fields, first_ref[k], second_ref[k], odd)
        if k < FSTEPS - 1:
            for q in range(2):
                trail_ref[k, q] = fields[q]
    for q in range(2):
        end_ref[q] = fields[q]
    far_means = window_means(fields, [far_ref[0], far_ref[1]], gather_ref[...])
    far_means_ref[...] = far_means
    start, end = [], []
    for q in range(2):
        moves = ((2 + q, 3, 7), (CF + 2 + q, 4, 0))
        start.append(place(near_start_ref[q], far_means, odd, moves))
        end.append(place(near_end_ref[q], far_means, odd, ((q, 2, 0), (CF + q, 3, 1))))
    sent = passed_on(end, start, first_group)
    for q in range(2):
        sent_ref[q] = sent[q][: 2 + 2 * EXT]
        ends_ref[q] = end[q]


def outer_kernel(
    among, far_ref, trail_ref, farther_ref, far_means_ref, gather_ref, sent_ref, near_ref, window_ref
):
    odd = lax.axis_index("space") % 2 == 1
    turn = jnp.where(odd, 1, ROWS - 1)
    group = lax.axis_index("tm")

    @pl.when(group >= among)
    def _():
        window_ref[...] = jnp.zeros_like(window_ref)

    @pl.when(group < among)
    def _():
        fields = [farther_ref[0], farther_ref[1]]
        for k in range(FSTEPS):
            beside = far_ref if k == 0 else trail_ref.at[k - 1]
            first = [pltpu.roll(beside[q], turn, 0) for q in range(2)]
            second = [pltpu.roll(first[q], turn, 0) for q in range(2)]
            fields = slanted(fields, first, second, odd)
        outer_means = window_means(fields, [farther_ref[0], farther_ref[1]], gather_ref[...])
        none = jnp.zeros((ROWS, outer_means.shape[1]), jnp.float32)
        gap = none[:2]
        start, end, window = [], [], []
        for q in range(2):
            begun = place(none, far_means_ref[...], odd, ((2 + q, 5, 1), (CF + 2 + q, 6, 2)))
            moves = ((2 + q, 7, 7), (CF + 2 + q, 0, 0))
            start.append(place(begun, outer_means, odd, moves))
            end.append(place(none, outer_means, odd, ((q, 6, 0), (CF + q, 7, 1))))
            beside = jnp.concatenate([near_ref[q], near_ref[q]], axis=0)
            middle = jnp.concatenate([gap, sent_ref[q], gap], axis=0)
            row = lax.broadcasted_iota(jnp.int32, none.shape, 0)
            window.append(jnp.where((row >= 2) & (row < 6), middle, beside))
        added = passed_on(end, start, group == 0)
        fresh = (row >= 6) == odd
        inside = (row >= 2) & (row < 6)
        for q in range(2):
            window_ref[q] = jnp.where(fresh & jnp.logical_not(inside), added[q], window[q])


def window_kernel(depth, own_ref, near_ref, far_ref, *rest):
    others, window_ref = rest[:-1], rest[-1]
    odd = lax.axis_index("space") % 2 == 1
    inner = own_ref.shape[1] - 2 * EXT
    for q in range(2):
        near, far = near_ref[q], far_ref[q]
        low, high = [jnp.where(odd, near, far)], [jnp.where(odd, far, near)]
        low += [others[2 * d][q] for d in range(depth - 1)]
        high += [others[2 * d + 1][q] for d in range(depth - 1)]
        parts = [low[-1][: EXT + inner]]
        parts += [part[EXT : EXT + inner] for part in reversed(low[:-1])]
        parts += [own_ref[q, EXT : EXT + inner]]
        parts += [part[EXT : EXT + inner] for part in high[:-1]]
        parts += [high[-1][EXT:]]
        window_ref[q] = jnp.concatenate(parts, axis=0)


def corrected(group, groups, held, kept_ref, end_ref, ends_ref, spread_ref, out_hbm, stage_ref, sems):
    reach = max(ref.shape[1] for ref in held)

    def placed(ref, q):
        term = ref[q]
        spare = (reach - term.shape[0]) // 2
        if spare:
            none = jnp.zeros((spare, term.shape[1]), jnp.float32)
            term = jnp.concatenate([none, term, none], axis=0)
        return term

    terms = [[placed(ref, q) for q in range(2)] for ref in held]

    def of(index):
        if index == groups - 1:
            return terms[0]
        picked = terms[min(len(terms) - 1, groups - 1 - index)]
        for k in range(min(len(terms) - 1, groups - 1 - index) - 1, -1, -1):
            picked = [jnp.where(group == index + k, terms[k][q], picked[q]) for q in range(2)]
        return picked

    path = of(0)
    for index in range(1, groups):
        term = of(index)
        after = advance(path, COARSE_COURANT, COARSE_DIFFUSION, 1)
        path = [jnp.where(index <= group, after[q] + term[q], path[q]) for q in range(2)]
    first = (reach - 2) // 2
    odd = lax.axis_index("space") % 2 == 1
    moves, own = [], []
    for q in range(2):
        move = path[q][first : first + 2] - ends_ref[q, EXT : EXT + 2]
        moves.append(repeat_rows(move[:1], move[1:]))
        upper = lax.broadcasted_iota(jnp.int32, kept_ref.shape[1:], 0) >= CF
        own.append(shifted(jnp.where(upper == odd, kept_ref[q], end_ref[q]), CF, 0))
    lifted = by_pieces(jnp.concatenate(moves, axis=0), spread_ref[...])
    copies = []
    width = out_hbm.shape[2] // OUT_PIECES
    for i in range(OUT_PIECES):
        cols = slice(i * width, (i + 1) * width)
        for q in range(2):
            stage_ref[q, :, cols] = own[q][:, cols] + lifted[q * ROWS : (q + 1) * ROWS, cols]
        copy = pltpu.make_async_copy(stage_ref.at[:, :, cols], out_hbm.at[:, :, cols], sems.at[i])
        copy.start()
        copies.append(copy)
    for copy in copies:
        copy.wait()


def early_kernel(among, kept_ref, end_ref, ends_ref, spread_ref, *rest):
    held, (out_hbm, stage_ref, sems) = rest[:-3], rest[-3:]
    group = lax.axis_index("tm")

    @pl.when(group < among)
    def _():
        corrected(
            group, among, held, kept_ref, end_ref, ends_ref, spread_ref, out_hbm, stage_ref, sems
        )


def late_kernel(groups, among, before_hbm, kept_ref, end_ref, ends_ref, spread_ref, *rest):
    held, (out_hbm, stage_ref, sems) = rest[:-3], rest[-3:]
    group = lax.axis_index("tm")

    @pl.when(group >= among)
    def _():
        corrected(
            group, groups, held, kept_ref, end_ref, ends_ref, spread_ref, out_hbm, stage_ref, sems
        )


def call(kernel, shapes, operands, cost=0, hbm=(), smem=(), scratch=(), out=VMEM, alias=None):
    where = [VMEM] * len(operands)
    for i in hbm:
        where[i] = pl.BlockSpec(memory_space=pl.ANY)
    for i in smem:
        where[i] = pl.BlockSpec(memory_space=pltpu.SMEM)
    return pl.pallas_call(
        kernel,
        out_shape=[jax.ShapeDtypeStruct(shape, dtype) for shape, dtype in shapes],
        in_specs=where,
        out_specs=[out] * len(shapes),
        input_output_aliases=alias or {},
        scratch_shapes=scratch,
        cost_estimate=pl.CostEstimate(flops=cost, bytes_accessed=cost // 8, transcendentals=0),
        compiler_params=pltpu.CompilerParams(vmem_limit_bytes=16 * 1024 * 1024),
    )(*operands)


def moved(block, axis, pairs):
    return lax.ppermute(block, axis, pairs)


def hold():
    at = lax.axis_index("space") % 4
    turns = jnp.where((at == 1) | (at == 2), HOLD_TURNS, 0)
    return lax.fori_loop(0, turns, lambda i, x: x * 1664525 + 1013904223, at)


def from_near(block):
    pairs = [(i, i ^ 1) for i in range(lax.axis_size("space"))]
    return moved(block, "space", pairs)


def from_far(block, step, among):
    count, groups = lax.axis_size("space"), lax.axis_size("tm")
    pairs = []
    for t in range(groups):
        for i in range(count):
            away = step if (i + step) % 2 == 0 else -step
            to = (i + away) % count if t < among else i ^ 1
            pairs.append((t * count + i, t * count + to))
    return moved(block, ("tm", "space"), pairs)


def forward(groups, count, distance):
    later = [(i + distance) % groups for i in range(groups)]
    if distance == 2 and groups > 2:
        later[-2:] = [1, 0]
    aside = 1 if 2 < distance == groups - 1 else -1
    return [
        (i * count + s, later[i] * count + (s ^ 1 if i == aside else s))
        for i in range(groups)
        for s in range(count)
    ]


def step(c_state):
    own = c_state[0]
    rows, cols = own.shape[1:]
    count, groups = lax.axis_size("space"), lax.axis_size("tm")
    assert rows == HALO == ROWS and count % 2 == 0
    full, half = jnp.float32, jnp.bfloat16
    inner, wide = rows // CF, cols // CF
    reach, among = groups - 1, groups - 1 - EXT
    depth = -(-(reach - EXT) // inner)
    held_back = hold()
    far = from_far(own, 1, groups)
    near = from_near(own)
    farther = from_far(own, 2, among) if depth == 1 else None
    own_here, own_sums, gather, spread = call(
        ready_kernel,
        [
            (own.shape, full),
            ((ROWS, cols), full),
            ((CF * LANES, LANES), half),
            ((LANES, CF * LANES), half),
        ],
        (held_back.reshape(1), own),
        cost=4_000_000,
        hbm=(1,),
        smem=(0,),
        scratch=[pltpu.SemaphoreType.DMA],
    )
    edges = ((FSTEPS, *own.shape), full)
    tile = ((2, ROWS, wide), full)
    first, second, kept, near_start, near_end = call(
        near_kernel,
        [edges, edges, (own.shape, full), tile, tile],
        (near, own_here, own_sums, gather),
        cost=8_000_000,
    )
    sent_shape = (2, inner + 2 * EXT, wide)
    end, sent, ends, trail, far_means = call(
        far_kernel,
        [
            (own.shape, full),
            (sent_shape, full),
            tile,
            ((FSTEPS - 1, *own.shape), full),
            ((ROWS, wide), full),
        ],
        (far, first, second, near_start, near_end, gather),
        cost=2_000_000,
    )
    near_rows = from_near(sent)
    window = ((2, inner * (2 * depth + 1) + 2 * EXT, wide), full)
    if depth == 1:
        (window,) = call(
            functools.partial(outer_kernel, among),
            [window],
            (far, trail, farther, far_means, gather, sent, near_rows),
            cost=2_000_000,
        )
    else:
        pieces = [sent, near_rows, from_far(sent, 1, among)]
        for d in range(2, depth + 1):
            for sign in (1, -1):
                pairs = [(i, (i + sign * d) % count) for i in range(count)]
                pieces.append(lax.ppermute(sent, "space", pairs))
        (window,) = call(functools.partial(window_kernel, depth), [window], pieces)
    held = [sent]
    for k in range(1, groups):
        held.append(moved(sent if k <= EXT else window, ("tm", "space"), forward(groups, count, k)))
    whole = (own.shape, full)
    scratch = [pltpu.VMEM(own.shape, full), pltpu.SemaphoreType.DMA((OUT_PIECES,))]
    early = min(groups, 1 + EXT)
    (after,) = call(
        functools.partial(early_kernel, early),
        [whole],
        (kept, end, ends, spread, *held[:early]),
        cost=1_000_000,
        scratch=scratch,
        out=pl.BlockSpec(memory_space=pltpu.HBM),
    )
    if groups > early:
        (after,) = call(
            functools.partial(late_kernel, groups, early),
            [whole],
            (after, kept, end, ends, spread, *held),
            cost=1_000_000,
            hbm=(0,),
            scratch=scratch,
            out=pl.BlockSpec(memory_space=pltpu.HBM),
            alias={0: 0},
        )
    return after[None]


def solution(mesh):
    placed = (P("tm", None, "space", None),)
    return jax.shard_map(
        step, mesh=mesh, in_specs=placed, out_specs=P("tm", None, "space", None), check_vma=False
    )
```
